32 devices in a mesh: band: 16 (over z, y, x), dp: 2 (over core).
Axes of the slice: x: 2, y: 2, z: 4, core: 2. Of those that a mesh axis runs over, the one named last changes fastest.
Arguments:
- pages: bfloat16 [32768, 256], P('band', 'dp'), may hold values from -6 to 6
- band_tiles: bfloat16 [256, 3, 128, 128], P('band'), may hold values from 0 to 1, as said below
- off_tiles: bfloat16 [256, 128, 128], P('band'), may hold values from 0 to 1, as said below
- off_row: int32 [256], P('band'), may hold values from 0 to 15
- requests: int32 [256], P('band'), may hold values from 0 to 15
- label_page: int32 [16384], P('band'), may hold values from 0 to 2047
- labels: int32 [16384], P(('band', 'dp')), may hold values from 0 to 255
- w_first: bfloat16 [768, 1024], replicated, may hold values from -0.21875 to 0.21875
- w_second: bfloat16 [1024, 256], replicated
Outputs:
- prop_a: bfloat16 [32768, 256], P('band', 'dp')
- prop_t: bfloat16 [32768, 256], P('band', 'dp')
- prop_aat: bfloat16 [32768, 256], P('band', 'dp')
- grad_w1: bfloat16 [768, 1024], replicated
- grad_w2: bfloat16 [1024, 256], replicated
The draws below stay inside these ranges and needn't reach their ends.
Inputs may be any that keep to these rules, and one draw needn't show every extreme that they name: `off_row`: row block within a band. `requests`: row block within a band. `band_tiles`: links weighted between 0 and 1, about half of the entries zero. `off_tiles`: links weighted between 0 and 1, about half of the entries zero.
All inputs are finite; a program needn't handle non-finite values.
Results may differ from the reference program's by a relative error of at most 0.011.
Values may be sent and summed in bfloat16 or wider, within the bound.
A program may use at most 128 MiB of HBM per device.

```python
import math
import jax
import jax.numpy as jnp
from jax import lax

F = 256
HID = 1024
CLASSES = 256
TILE = 128
P_DEV = 2048
LAB_DEV = 1024
IN_F = 768
NB = 16
PAGES = 32768
BLOCKS = 256
OFFS = 256
LABELS = 16384
N_BAND = 16


def link_weights(key, shape):
    key_mask = jax.random.fold_in(key, 11)
    key_value = jax.random.fold_in(key, 12)
    present = jax.random.bernoulli(key_mask, 0.5, shape).astype(jnp.float32)
    values = jnp.exp(jax.random.uniform(key_value, shape, jnp.float32, math.log(0.02), math.log(0.12)))
    return present * values


def draw_band_tiles(key, part):
    return link_weights(key, (BLOCKS, 3, TILE, TILE)).astype(jnp.bfloat16)


def draw_off_tiles(key, part):
    return link_weights(key, (OFFS, TILE, TILE)).astype(jnp.bfloat16)


def draw_w_second(key, part):
    key_base = jax.random.fold_in(key, 21)
    values = jnp.clip(jax.random.normal(key_base, (HID, CLASSES), jnp.float32), -6.0, 6.0) * HID ** (-0.5)
    return values.astype(jnp.bfloat16)


def touch_ends(drawn, stream_key, smallest, largest):
    longest = drawn.shape.index(max(drawn.shape))
    spots = []
    for shift in (0, 1):
        where = [jax.random.randint(jax.random.fold_in(stream_key, axis), (), 0, length) for axis, length in enumerate(drawn.shape)]
        where[longest] = (where[longest] + shift) % drawn.shape[longest]
        spots.append(tuple(where))
    return drawn.at[spots[0]].set(smallest).at[spots[1]].set(largest)


def block_scale(stream_key, extent, pieces, least, top_value):
    factor_of, own = 1.0, jax.random.fold_in(stream_key, 6)
    for position, shards_of in pieces:
        draws = jnp.exp(jax.random.uniform(jax.random.fold_in(own, position), (shards_of,), jnp.float32, least / len(pieces), top_value / len(pieces)))
        factor_of = factor_of * jnp.repeat(draws, extent[position] // shards_of).reshape([-1 if axis == position else 1 for axis in range(len(extent))])
    return factor_of


def gaussian(own_key, extent, width, most, cuts=(), held_as=jnp.bfloat16):
    gain = block_scale(own_key, extent, cuts, -0.22, 0.18) if cuts else 1.0
    array = jax.random.normal(own_key, extent, jnp.float32) * width * gain
    return jnp.minimum(jnp.maximum(array, -most), most).astype(held_as)


def setup_inputs(seed: int = 0) -> dict:
    streams_of = jax.random.split(jax.random.key(seed), 10)
    return {
        "pages": gaussian(streams_of[0], (PAGES, F), 1.0, 6.0, ((0, 16), (1, 2))),
        "band_tiles": draw_band_tiles(jax.random.fold_in(streams_of[9], 71), 0),
        "off_tiles": draw_off_tiles(jax.random.fold_in(streams_of[9], 71), 0),
        "off_row": touch_ends(jax.random.randint(streams_of[3], (OFFS,), 0, NB), jax.random.fold_in(streams_of[3], 1), 0, NB - 1).astype(jnp.int32),
        "requests": touch_ends(jax.random.randint(streams_of[4], (OFFS,), 0, NB), jax.random.fold_in(streams_of[4], 1), 0, NB - 1).astype(jnp.int32),
        "label_page": touch_ends(jax.random.randint(streams_of[5], (LABELS,), 0, P_DEV), jax.random.fold_in(streams_of[5], 1), 0, P_DEV - 1).astype(jnp.int32),
        "labels": touch_ends(jax.random.randint(streams_of[6], (LABELS,), 0, CLASSES), jax.random.fold_in(streams_of[6], 1), 0, CLASSES - 1).astype(jnp.int32),
        "w_first": gaussian(streams_of[7], (IN_F, HID), IN_F ** -0.5, 0.21875),
        "w_second": draw_w_second(jax.random.fold_in(streams_of[9], 71), 0),
    }


def band_forward(band_tiles, field):
    block_count = P_DEV // TILE
    v_blocks = field.reshape(N_BAND * block_count, TILE, F)
    zero_block = jnp.zeros((1, TILE, F), field.dtype)
    padded = jnp.concatenate([zero_block, v_blocks, zero_block], 0)
    band_set = band_tiles.reshape(N_BAND, block_count, 3, TILE, TILE)

    def per_device(device_id):
        window = lax.dynamic_slice_in_dim(padded, device_id * block_count, block_count + 2, 0)
        windows = jnp.stack([window[0:block_count], window[1:block_count + 1], window[2:block_count + 2]], 1)
        tiles_here = lax.dynamic_index_in_dim(band_set, device_id, 0, keepdims=False)
        return jnp.einsum('rjab,rjbf->raf', tiles_here.astype(jnp.float32), windows.astype(jnp.float32),
                          precision=lax.Precision.HIGHEST)

    result = lax.map(per_device, jnp.arange(N_BAND, dtype=jnp.int32))
    return result.reshape(PAGES, F)


def band_adjoint(band_tiles, field):
    block_count = P_DEV // TILE
    v_blocks = field.reshape(N_BAND, block_count, TILE, F)
    band_set = band_tiles.reshape(N_BAND, block_count, 3, TILE, TILE)

    def per_device(pair):
        tiles_here, blocks_here = pair
        adjoint_terms = jnp.einsum('rjab,raf->rjbf', tiles_here.astype(jnp.float32), blocks_here.astype(jnp.float32),
                                   precision=lax.Precision.HIGHEST)
        accumulated = jnp.zeros((block_count + 2, TILE, F), jnp.float32)
        accumulated = accumulated.at[0:block_count].add(adjoint_terms[:, 0])
        accumulated = accumulated.at[1:block_count + 1].add(adjoint_terms[:, 1])
        accumulated = accumulated.at[2:block_count + 2].add(adjoint_terms[:, 2])
        return accumulated

    accumulated = lax.map(per_device, (band_set, v_blocks))
    inner_part = accumulated[:, 1:block_count + 1]
    low_rim = accumulated[:, 0]
    high_rim = accumulated[:, block_count + 1]
    from_right = jnp.concatenate([low_rim[1:], jnp.zeros_like(low_rim[:1])], 0)
    from_left = jnp.concatenate([jnp.zeros_like(high_rim[:1]), high_rim[:-1]], 0)
    inner_part = inner_part.at[:, block_count - 1].add(from_right)
    inner_part = inner_part.at[:, 0].add(from_left)
    return inner_part.reshape(PAGES, F)


def off_forward(off_tiles, off_row, requests, field):
    block_count = P_DEV // TILE
    v_blocks = field.reshape(N_BAND * block_count, TILE, F)
    tile_set = off_tiles.reshape(N_BAND, N_BAND, TILE, TILE)
    row_ids = off_row.reshape(N_BAND, N_BAND)
    request_ids = requests.reshape(N_BAND, N_BAND)
    peer_base = jnp.arange(N_BAND, dtype=jnp.int32) * block_count

    def per_device(triple):
        tiles_here, rows_here, wanted = triple
        columns = (peer_base + wanted).astype(jnp.int32)
        fetched = v_blocks[columns]
        products = jnp.einsum('kab,kbf->kaf', tiles_here.astype(jnp.float32), fetched.astype(jnp.float32),
                              precision=lax.Precision.HIGHEST)
        row_hot = (rows_here[None, :] == jnp.arange(block_count, dtype=jnp.int32)[:, None]).astype(jnp.float32)
        return jnp.einsum('rk,kaf->raf', row_hot, products, precision=lax.Precision.HIGHEST)

    result = lax.map(per_device, (tile_set, row_ids, request_ids))
    return result.reshape(PAGES, F)


def off_adjoint(off_tiles, off_row, requests, field):
    block_count = P_DEV // TILE
    v_blocks = field.reshape(N_BAND * block_count, TILE, F)
    tile_set = off_tiles.reshape(N_BAND, N_BAND, TILE, TILE)
    row_ids = off_row.reshape(N_BAND, N_BAND)
    request_ids = requests.reshape(N_BAND, N_BAND)
    peer_base = jnp.arange(N_BAND, dtype=jnp.int32) * block_count

    def step_fn(total, quad):
        device_id, tiles_here, rows_here, wanted = quad
        sources = v_blocks[(device_id * block_count + rows_here).astype(jnp.int32)]
        term_block = jnp.einsum('kab,kaf->kbf', tiles_here.astype(jnp.float32), sources.astype(jnp.float32),
                                precision=lax.Precision.HIGHEST)
        term_block = lax.optimization_barrier(term_block.astype(jnp.bfloat16)).astype(jnp.float32)
        columns = (peer_base + wanted).astype(jnp.int32)
        return total.at[columns].add(term_block), None

    start = jnp.zeros((N_BAND * block_count, TILE, F), jnp.float32)
    total, _ = lax.scan(step_fn, start, (jnp.arange(N_BAND, dtype=jnp.int32), tile_set, row_ids, request_ids))
    return total.reshape(PAGES, F)


def reference(pages, band_tiles, off_tiles, off_row, requests, label_page, labels, w_first, w_second):
    prop_a = (band_forward(band_tiles, pages) + off_forward(off_tiles, off_row, requests, pages)).astype(jnp.bfloat16)
    prop_t = (band_adjoint(band_tiles, pages) + off_adjoint(off_tiles, off_row, requests, pages)).astype(jnp.bfloat16)
    prop_aat = (band_forward(band_tiles, prop_t) + off_forward(off_tiles, off_row, requests, prop_t)).astype(jnp.bfloat16)
    global_rows = ((jnp.arange(LABELS, dtype=jnp.int32) // LAB_DEV) * P_DEV + label_page).astype(jnp.int32)
    features = jnp.concatenate([prop_a[global_rows], prop_t[global_rows], prop_aat[global_rows]], 1)
    pre_act = jnp.dot(features, w_first, preferred_element_type=jnp.float32)
    sigma = jax.nn.sigmoid(pre_act)
    hidden = (pre_act * sigma).astype(jnp.bfloat16)
    logits = jnp.dot(hidden, w_second, preferred_element_type=jnp.float32)
    probabilities = jax.nn.softmax(logits, axis=-1)
    label_hot = (labels[:, None] == jnp.arange(CLASSES, dtype=jnp.int32)[None, :]).astype(jnp.float32)
    errors = ((probabilities - label_hot) / LAB_DEV).astype(jnp.bfloat16)
    grad_w2 = jnp.dot(hidden.T, errors, preferred_element_type=jnp.float32).astype(jnp.bfloat16)
    slope = sigma * (1.0 + pre_act * (1.0 - sigma))
    back_signal = (jnp.dot(errors, w_second.T, preferred_element_type=jnp.float32) * slope).astype(jnp.bfloat16)
    grad_w1 = jnp.dot(features.T, back_signal, preferred_element_type=jnp.float32).astype(jnp.bfloat16)
    return prop_a, prop_t, prop_aat, grad_w1, grad_w2
```

```python
import functools

import jax
import jax.numpy as jnp
from jax import lax
from jax.experimental import pallas as pl
from jax.experimental.pallas import tpu as pltpu
from jax.sharding import PartitionSpec as P


MESH = pl.DeviceIdType.MESH


def greet(n):
    b, other = lax.axis_index("band"), 1 - lax.axis_index("dp")
    barrier = pltpu.get_barrier_semaphore()
    pl.semaphore_signal(barrier, inc=1, device_id={"dp": other}, device_id_type=MESH)

    def call(d, _):
        pl.semaphore_signal(
            barrier, inc=1, device_id={"band": lax.rem(b + d, n)}, device_id_type=MESH
        )
        return 0

    lax.fori_loop(1, n, call, 0)


def met(n):
    pl.semaphore_wait(pltpu.get_barrier_semaphore(), n)


def remote(src, dst, send_sem, recv_sem, **where):
    return pltpu.make_async_remote_copy(
        src_ref=src, dst_ref=dst, send_sem=send_sem, recv_sem=recv_sem,
        device_id=where, device_id_type=MESH,
    )


def each(start, stop, body):
    def step(d, _):
        body(d)
        return 0

    lax.fori_loop(start, stop, step, 0)


def reduce_kernel(
    g, depth, pieces, by_rows, feats, mine, w1, w2, label, out,
    feat_t, hid, hid_in, err, back, slope, cur, q1s, q1r, q2s, q2r, q3s, q3r,
    s_act, r_act, s_back, r_back, s_one, r_one, s_two, r_two, s_z, r_z,
    s_gz, r_gz, s_g2, r_g2, s_g1, r_g1, s_fw, r_fw,
):
    n = g * g * depth
    b, h = lax.axis_index("band"), lax.axis_index("dp")
    o = 1 - h
    x, y, z = lax.rem(b, g), lax.rem(lax.div(b, g), g), lax.div(b, g * g)
    c1, c2 = x + h * (y - x), y + h * (x - y)
    stride1, stride2 = 1 + h * (g - 1), g - h * (g - 1)
    count, classes = feats.shape[0], w2.shape[1]
    picks, _, fh = mine.shape
    half, width = cur.shape[1:]
    low = hid_in.shape[1]
    top = picks * fh
    quarter = half - top
    low_step = low // pieces
    rows1 = half // g
    rows2 = rows1 // g
    base1 = c1 * rows1
    base2 = base1 + c2 * rows2
    tall, thin = (rows2 // depth, width) if by_rows else (rows2, width // depth)
    f32, bf16, i16 = jnp.float32, jnp.bfloat16, jnp.int16
    fine = 14.0

    def down(start, size):
        return pl.ds(pl.multiple_of(start, 16), size)

    def across(start, size):
        return pl.ds(pl.multiple_of(start, 128), size)

    def member1(d):
        m = lax.rem(c1 + d, g)
        return m, b + (m - c1) * stride1

    def member2(d):
        m = lax.rem(c2 + d, g)
        return m, b + (m - c2) * stride2

    def member_z(d):
        m = lax.rem(z + d, depth)
        return m, b + (m - z) * (g * g)

    def spot_z(m):
        if by_rows:
            return down(base2 + m * tall, tall), pl.ds(0, width)
        return down(base2, rows2), across(m * thin, thin)

    def encode(value, ref):
        rows, cols = value.shape
        most = jnp.max(jnp.abs(value), axis=0, keepdims=True)
        power = jnp.floor(jnp.log2(jnp.maximum(most, 1e-33))) + 1.0
        whole = jnp.round(value * jnp.exp2(fine - power)).astype(jnp.int32)
        ref[:rows] = whole.astype(i16)
        ref[rows:] = jnp.broadcast_to(power, (16, cols)).astype(jnp.int32).astype(i16)

    def decode(ref):
        rows = ref.shape[0] - 16
        power = ref[rows:].astype(jnp.int32).astype(f32)[:1]
        return ref[:rows].astype(jnp.int32).astype(f32) * jnp.exp2(power - fine)

    def act_copies():
        return (
            remote(hid.at[:, across(o * low, low)], hid_in, s_act.at[0], r_act.at[0], dp=o),
            remote(err.at[0], err.at[1], s_act.at[1], r_act.at[1], dp=o),
        )

    def back_copy(p):
        return remote(back.at[p, 0], back.at[p, 1], s_back.at[p], r_back.at[p], dp=o)

    def one(p, d):
        return remote(
            q1s.at[p, d - 1], q1r.at[p, d - 1], s_one.at[p, d - 1], r_one.at[p, d - 1],
            band=member1(d)[1],
        )

    def two(p, d):
        return remote(
            q2s.at[p, d - 1], q2r.at[p, d - 1], s_two.at[p, d - 1], r_two.at[p, d - 1],
            band=member2(d)[1],
        )

    def along_z(p, d):
        return remote(
            q3s.at[p, d - 1], q3r.at[p, d - 1], s_z.at[p, d - 1], r_z.at[p, d - 1],
            band=member_z(d)[1],
        )

    def back_z(p, d, taking=False):
        m, t = member_z(d)
        owner = lax.rem(z + depth - d, depth) if taking else z
        rows, cols = spot_z(owner)
        spot = out.at[h, p, rows, cols]
        return remote(spot, spot, s_gz.at[p, d - 1], r_gz.at[p, d - 1], band=t)

    def back2(p, d, taking=False):
        m, t = member2(d)
        owner = lax.rem(c2 + g - d, g) if taking else c2
        spot = out.at[h, p, down(base1 + owner * rows2, rows2)]
        return remote(spot, spot, s_g2.at[p, d - 1], r_g2.at[p, d - 1], band=t)

    def back1(p, d, taking=False):
        m, t = member1(d)
        owner = lax.rem(c1 + g - d, g) if taking else c1
        spot = out.at[h, p, down(owner * rows1, rows1)]
        return remote(spot, spot, s_g1.at[p, d - 1], r_g1.at[p, d - 1], band=t)

    def forward(p, core):
        spot = out.at[core, p]
        return remote(spot, spot, s_fw.at[p], r_fw.at[p], dp=o)

    def dot(lhs, rhs, i, j):
        return lax.dot_general(lhs, rhs, (((i,), (j,)), ((), ())), preferred_element_type=f32)

    def errors_back(p):
        w = slice(p * width, (p + 1) * width)
        signal = dot(err[0], w2[w], 1, 1) * slope[:, w]
        back[p, 0] = signal.astype(bf16)
        back_copy(p).start()

    def gradients(p):
        back_copy(p).wait_recv()
        cur[p, :top] = dot(feat_t[...], back[p].reshape(2 * count, width), 1, 0)
        if p == 0:
            for copy in act_copies():
                copy.wait_recv()
        for j in range(low_step // quarter):
            start = p * low_step + j * quarter
            cur[p, top:, j * classes : (j + 1) * classes] = dot(
                hid[:, across(h * low + start, quarter)], err[0], 0, 0
            ) + dot(hid_in[:, start : start + quarter], err[1], 0, 0)
        for d in range(1, g):
            encode(cur[p, down(member1(d)[0] * rows1, rows1)], q1s.at[p, d - 1])
            one(p, d).start()

    def after_one(p):
        for d in range(1, g):
            one(p, d).wait_recv()
            cur[p, down(base1, rows1)] += decode(q1r.at[p, d - 1])
        for d in range(1, g):
            encode(cur[p, down(base1 + member2(d)[0] * rows2, rows2)], q2s.at[p, d - 1])
            two(p, d).start()

    def after_two(p):
        for d in range(1, g):
            two(p, d).wait_recv()
            cur[p, down(base2, rows2)] += decode(q2r.at[p, d - 1])
        for d in range(1, depth):
            rows, cols = spot_z(member_z(d)[0])
            encode(cur[p, rows, cols], q3s.at[p, d - 1])
            along_z(p, d).start()

    def after_z(p):
        rows, cols = spot_z(z)
        total = cur[p, rows, cols]
        for d in range(1, depth):
            along_z(p, d).wait_recv()
            total += decode(q3r.at[p, d - 1])
        out[h, p, rows, cols] = total.astype(bf16)
        for d in range(1, depth):
            back_z(p, d).start()

    def after_back_z(p):
        for d in range(1, depth):
            back_z(p, d, True).wait_recv()
        for d in range(1, g):
            back2(p, d).start()

    def after_back2(p):
        for d in range(1, g):
            back2(p, d, True).wait_recv()
        for d in range(1, g):
            back1(p, d).start()

    def after_back1(p):
        for d in range(1, g):
            back1(p, d, True).wait_recv()
        forward(p, h).start()

    span = label.shape[2]
    lane = lax.broadcasted_iota(jnp.int32, (span, span), 1)
    greet(n)
    step = min(width, 256)
    for c in range(hid.shape[1] // step):
        w = slice(c * step, (c + 1) * step)
        pre = dot(feats[...], w1[:, w], 1, 0)
        sigma = jax.nn.sigmoid(pre)
        hid[:, w] = (pre * sigma).astype(bf16)
        slope[:, w] = sigma * (1.0 + pre * (1.0 - sigma))
    for i in range(count // span):
        rows = slice(i * span, (i + 1) * span)
        logits = dot(hid[rows], w2[...], 1, 0)
        powers = jnp.exp(logits - jnp.max(logits, axis=-1, keepdims=True))
        shares = powers / jnp.sum(powers, axis=-1, keepdims=True)
        wanted = jnp.broadcast_to(label[i], (span, span)).T
        label_hot = jnp.concatenate(
            [jnp.where(wanted == lane + c * span, 1.0, 0.0) for c in range(classes // span)], axis=1
        )
        err[0, rows] = ((shares - label_hot) / (2 * count)).astype(bf16)
    met(n)
    for copy in act_copies():
        copy.start()
    for j in range(picks):
        own = feats[:, across((2 * j + h) * fh, fh)]
        feat_t[j * fh : (j + 1) * fh, :count] = own.T
        feat_t[j * fh : (j + 1) * fh, count:] = mine[j].T
    stages = (
        errors_back, gradients, after_one, after_two, after_z, after_back_z, after_back2, after_back1
    )
    for t in range(len(stages) + pieces - 1):
        for p in reversed(range(pieces)):
            if 0 <= t - p < len(stages):
                stages[t - p](p)
    for copy in act_copies():
        copy.wait_send()
    for p in range(pieces):
        back_copy(p).wait_send()
        for d in range(1, g):
            for copy in (one(p, d), two(p, d), back2(p, d), back1(p, d)):
                copy.wait_send()
        for d in range(1, depth):
            along_z(p, d).wait_send()
            back_z(p, d).wait_send()
        forward(p, h).wait_send()
        forward(p, o).wait_recv()


def hand_out(top, fh, packed, a, t, aat, out_a, out_t, out_aat, grad1, grad2, sem):
    _, pieces, half, width = packed.shape
    classes = grad2.shape[1]
    quarter = half - top
    groups = width // classes
    copies = [
        pltpu.make_async_copy(source, target, sem.at[i])
        for i, (source, target) in enumerate(((a, out_a), (t, out_t), (aat, out_aat)))
    ]
    for core in range(2):
        for p in range(pieces):
            for j in range(top // fh):
                copies.append(
                    pltpu.make_async_copy(
                        packed.at[core, p, pl.ds(j * fh, fh)],
                        grad1.at[pl.ds((2 * j + core) * fh, fh), pl.ds(p * width, width)],
                        sem.at[len(copies)],
                    )
                )
            for j in range(groups):
                start = ((core * pieces + p) * groups + j) * quarter
                copies.append(
                    pltpu.make_async_copy(
                        packed.at[core, p, pl.ds(top, quarter), pl.ds(j * classes, classes)],
                        grad2.at[pl.ds(start, quarter)],
                        sem.at[len(copies)],
                    )
                )
    for copy in copies:
        copy.start()
    for copy in copies:
        copy.wait()


def summed_gradients(features, mine, w_first, w_second, labels):
    n = lax.axis_size("band")
    g = max(1, round((n / 2) ** (1 / 3)))
    if n % (g * g):
        g = 1
    depth = n // (g * g)
    hid, classes = w_second.shape
    picks, count, fh = mine.shape
    top, low = picks * fh, hid // 2
    half = (w_first.size + w_second.size) // (2 * hid)
    rows2 = half // (g * g)
    by_rows = rows2 % (16 * depth) == 0
    pieces = max(1, hid // 256 if by_rows else hid // (128 * depth))
    width = hid // pieces
    f32, bf16, i16 = jnp.float32, jnp.bfloat16, jnp.int16
    tall, thin = (rows2 // depth, width) if by_rows else (rows2, width // depth)
    vmem = pl.BlockSpec(memory_space=pltpu.VMEM)
    dma = pltpu.SemaphoreType.DMA
    side, deep = max(1, g - 1), max(1, depth - 1)
    near, far = dma((pieces, side)), dma((pieces, deep))
    first = pltpu.VMEM((pieces, side, half // g + 16, width), i16)
    second = pltpu.VMEM((pieces, side, rows2 + 16, width), i16)
    third = pltpu.VMEM((pieces, deep, tall + 16, thin), i16)
    return pl.pallas_call(
        functools.partial(reduce_kernel, g, depth, pieces, by_rows),
        out_shape=jax.ShapeDtypeStruct((2, pieces, half, width), bf16),
        in_specs=[vmem] * 5,
        out_specs=vmem,
        scratch_shapes=[
            pltpu.VMEM((top, 2 * count), bf16),
            pltpu.VMEM((count, hid), bf16),
            pltpu.VMEM((count, low), bf16),
            pltpu.VMEM((2, count, classes), bf16),
            pltpu.VMEM((pieces, 2, count, width), bf16),
            pltpu.VMEM((count, hid), f32),
            pltpu.VMEM((pieces, half, width), f32),
            first, first, second, second, third, third,
            dma((2,)), dma((2,)), dma((pieces,)), dma((pieces,)),
            near, near, near, near, far, far, far, far, near, near, near, near,
            dma((pieces,)), dma((pieces,)),
        ],
        compiler_params=pltpu.CompilerParams(
            collective_id=0, has_side_effects=True, vmem_limit_bytes=40 * 2**20
        ),
        name="grad_sum",
    )(features, mine, w_first, w_second, labels.reshape(count // 128, 1, 128))


def handed_out(packed, prop_a, prop_t, prop_aat, w_first, w_second, fh):
    top = w_first.shape[0] // 2
    _, pieces, half, width = packed.shape
    groups = width // w_second.shape[1]
    total = 3 + 2 * pieces * (top // fh + groups)
    vmem = pl.BlockSpec(memory_space=pltpu.VMEM)
    anywhere = pl.BlockSpec(memory_space=pl.ANY)
    return pl.pallas_call(
        functools.partial(hand_out, top, fh),
        out_shape=tuple(
            jax.ShapeDtypeStruct(a.shape, a.dtype)
            for a in (prop_a, prop_t, prop_aat, w_first, w_second)
        ),
        in_specs=[vmem, anywhere, anywhere, anywhere],
        out_specs=(anywhere,) * 5,
        scratch_shapes=[pltpu.SemaphoreType.DMA((total,))],
        name="hand_out",
    )(packed, prop_a, prop_t, prop_aat)


def propagate_kernel(
    n, pages, tiles, offs, off_row, req, label, prop_a, prop_t, prop_aat, feats, sel,
    hot, back_send, back_land, page_send, page_land, t_send, t_land, pad, padt,
    rim_send, rim_land, inner, acc, req_out, req_land, served, local_sem,
    s_req, r_req, s_back, r_back, s_page, r_page, s_t, r_t, s_edge, r_edge, s_pick, r_pick,
):
    b, h = lax.axis_index("band"), lax.axis_index("dp")
    o = 1 - h
    nb, tile, fh = pages.shape
    left, right = lax.rem(b + n - 1, n), lax.rem(b + 1, n)
    half = feats.shape[0]
    f32, bf16 = jnp.float32, jnp.bfloat16

    def ahead(d):
        return lax.rem(b + d, n)

    def behind(d):
        return lax.rem(b + n - d, n)

    def tdot(x, y):
        return lax.dot_general(x, y, (((0,), (0,)), ((), ())), preferred_element_type=f32)

    def dot(x, y):
        return jnp.dot(x, y, preferred_element_type=f32)

    barrier = pltpu.get_barrier_semaphore()
    pl.semaphore_signal(barrier, inc=1, device_id={"dp": o}, device_id_type=MESH)
    each(
        1,
        n,
        lambda d: pl.semaphore_signal(
            barrier, inc=1, device_id={"band": ahead(d)}, device_id_type=MESH
        ),
    )
    chunk = label.shape[2]
    lane = lax.broadcasted_iota(jnp.int32, (chunk, chunk), 1)

    def build_hot(i):
        rows = pl.ds(pl.multiple_of(i * chunk, chunk), chunk)
        wanted = jnp.broadcast_to(label[i], (chunk, chunk)).T
        for c in range(nb * tile // chunk):
            hot[rows, c * chunk : (c + 1) * chunk] = jnp.where(
                wanted == lane + c * chunk, 1.0, 0.0
            ).astype(bf16)

    def build_req(t):
        req_out[t] = jnp.full((1, 128), req[t], jnp.int32)

    each(0, n, build_req)
    each(0, hot.shape[0] // chunk, build_hot)
    rim_send[0] = tdot(tiles[0, 0], pages[0])
    rim_send[1] = tdot(tiles[nb - 1, 2], pages[nb - 1])
    pl.semaphore_wait(barrier, n)

    def ask(d):
        t = ahead(d)
        return remote(req_out.at[t], req_land.at[d], s_req.at[d], r_req.at[d], band=t)

    def send_back(d):
        return remote(back_send.at[d], back_land.at[d], s_back.at[d], r_back.at[d], band=ahead(d))

    def send_page(d):
        return remote(page_send.at[d], page_land.at[d], s_page.at[d], r_page.at[d], band=behind(d))

    def send_t(d):
        return remote(t_send.at[d], t_land.at[d], s_t.at[d], r_t.at[d], band=behind(d))

    def edges(source, field, i):
        first, last = source
        return (
            remote(first, field.at[nb + 1], s_edge.at[i], r_edge.at[i], band=left),
            remote(last, field.at[0], s_edge.at[i + 1], r_edge.at[i + 1], band=right),
        )

    each(1, n, lambda d: ask(d).start())
    rims = (
        remote(rim_send.at[0], rim_land.at[0], s_edge.at[2], r_edge.at[2], band=left),
        remote(rim_send.at[1], rim_land.at[1], s_edge.at[3], r_edge.at[3], band=right),
    )
    page_edges = edges((pages.at[0], pages.at[nb - 1]), pad, 0)
    for copy in rims + page_edges:
        copy.start()

    def back_term(d):
        k = ahead(d)
        return tdot(offs[k], pages[off_row[k]]).astype(bf16)

    def make_back(d):
        back_send[d] = back_term(d)
        send_back(d).start()

    each(1, n, make_back)
    back_land[0] = back_term(0)
    req_land[0] = req_out[b]
    each(1, n, lambda d: ask(d).wait_recv())
    to_scalar = pltpu.make_async_copy(req_land, served, local_sem.at[0])
    to_scalar.start()
    to_scalar.wait()

    def make_page(d):
        page_send[d] = pages[served[d, 0, 0]]
        send_page(d).start()

    each(1, n, make_page)
    page_land[0] = pages[served[0, 0, 0]]

    inner[0] = tdot(tiles[0, 1], pages[0]) + tdot(tiles[1, 0], pages[1])
    inner[nb - 1] = tdot(tiles[nb - 1, 1], pages[nb - 1]) + tdot(tiles[nb - 2, 2], pages[nb - 2])

    def adjoint(m):
        inner[m] = (
            tdot(tiles[m - 1, 2], pages[m - 1])
            + tdot(tiles[m, 1], pages[m])
            + tdot(tiles[m + 1, 0], pages[m + 1])
        )

    each(1, nb - 1, adjoint)
    for copy in rims:
        copy.wait()
    inner[nb - 1] += jnp.where(b < n - 1, 1.0, 0.0) * rim_land[0]
    inner[0] += jnp.where(b > 0, 1.0, 0.0) * rim_land[1]

    def spread_rows(target, spot, term):
        for r in range(nb):
            target[r] += jnp.where(spot == r, 1.0, 0.0) * term

    def take_back(d):
        spread_rows(inner, served[d, 0, 0], back_land[d].astype(f32))

    take_back(0)

    def await_back(d):
        send_back(d).wait_recv()
        take_back(d)

    each(1, n, await_back)

    def round_t(r):
        block = inner[r].astype(bf16)
        padt[r + 1] = block
        prop_t[r] = block

    each(0, nb, round_t)
    t_edges = edges((padt.at[1], padt.at[nb]), padt, 4)
    for copy in t_edges:
        copy.start()

    def make_t(d):
        t_send[d] = prop_t[served[d, 0, 0]]
        send_t(d).start()

    each(1, n, make_t)
    t_land[0] = prop_t[served[0, 0, 0]]

    def copy_pages(r):
        pad[r + 1] = pages[r]

    each(0, nb, copy_pages)

    def clear_ends(field):
        @pl.when(b == 0)
        def _():
            field[0] = jnp.zeros((tile, fh), bf16)

        @pl.when(b == n - 1)
        def _():
            field[nb + 1] = jnp.zeros((tile, fh), bf16)

    def near(field):
        def row(r):
            weights = jnp.concatenate([tiles[r, 0], tiles[r, 1], tiles[r, 2]], axis=1)
            window = jnp.concatenate([field[r], field[r + 1], field[r + 2]], axis=0)
            acc[r] = dot(weights, window)

        each(0, nb, row)

    def take_off(land, d):
        k = ahead(d)
        spread_rows(acc, off_row[k], dot(offs[k], land[d]))

    def pick(j, field):
        whole = field[1 : nb + 1].reshape(nb * tile, fh)
        step = half // 2

        def rows_of(core, c):
            return pl.ds(pl.multiple_of(core * half + c * step, step), step)

        columns = pl.ds(pl.multiple_of((2 * j + h) * fh, fh), fh)
        for c in range(2):
            sel[j, c * step : (c + 1) * step] = dot(hot[rows_of(o, c)], whole).astype(bf16)
        give = remote(sel.at[j], feats.at[:, columns], s_pick.at[j], r_pick.at[j], dp=o)
        give.start()
        for c in range(2):
            feats[c * step : (c + 1) * step, columns] = dot(hot[rows_of(h, c)], whole).astype(bf16)
        return give

    gives = [pick(1, padt)]
    for copy in page_edges:
        copy.wait()
    clear_ends(pad)
    near(pad)
    take_off(page_land, 0)

    def await_page(d):
        send_page(d).wait_recv()
        take_off(page_land, d)

    each(1, n, await_page)

    def round_a(r):
        block = acc[r].astype(bf16)
        pad[r + 1] = block
        prop_a[r] = block

    each(0, nb, round_a)
    gives.append(pick(0, pad))
    for copy in t_edges:
        copy.wait()
    clear_ends(padt)
    near(padt)
    take_off(t_land, 0)

    def await_t(d):
        send_t(d).wait_recv()
        take_off(t_land, d)

    each(1, n, await_t)

    def round_aat(r):
        block = acc[r].astype(bf16)
        padt[r + 1] = block
        prop_aat[r] = block

    each(0, nb, round_aat)
    gives.append(pick(2, padt))

    def finish(d):
        ask(d).wait_send()
        send_back(d).wait_send()
        send_page(d).wait_send()
        send_t(d).wait_send()

    each(1, n, finish)
    for j, give in zip((1, 0, 2), gives):
        give.wait_send()
        columns = pl.ds(pl.multiple_of((2 * j + o) * fh, fh), fh)
        remote(
            sel.at[j], feats.at[:, columns], s_pick.at[j], r_pick.at[j], dp=o
        ).wait_recv()


def propagated(pages, band_tiles, off_tiles, off_row, requests, label_page):
    n = lax.axis_size("band")
    tile = band_tiles.shape[-1]
    rows, fh = pages.shape
    nb = rows // tile
    count = label_page.shape[0]
    bf16, f32 = jnp.bfloat16, jnp.float32
    vmem = pl.BlockSpec(memory_space=pltpu.VMEM)
    smem = pl.BlockSpec(memory_space=pltpu.SMEM)
    dma = pltpu.SemaphoreType.DMA
    blocks = jax.ShapeDtypeStruct((nb, tile, fh), bf16)
    per_band = pltpu.VMEM((n, tile, fh), bf16)
    padded = pltpu.VMEM((nb + 2, tile, fh), bf16)
    half = count // 2
    prop_a, prop_t, prop_aat, feats, sel = pl.pallas_call(
        functools.partial(propagate_kernel, n),
        out_shape=(
            blocks, blocks, blocks,
            jax.ShapeDtypeStruct((half, 6 * fh), bf16),
            jax.ShapeDtypeStruct((3, half, fh), bf16),
        ),
        in_specs=[vmem, vmem, vmem, smem, smem, vmem],
        out_specs=(vmem,) * 5,
        scratch_shapes=[
            pltpu.VMEM((count, rows), bf16),
            per_band, per_band, per_band, per_band, per_band, per_band,
            padded, padded,
            pltpu.VMEM((2, tile, fh), f32),
            pltpu.VMEM((2, tile, fh), f32),
            pltpu.VMEM((nb, tile, fh), f32),
            pltpu.VMEM((nb, tile, fh), f32),
            pltpu.VMEM((n, 1, 128), jnp.int32),
            pltpu.VMEM((n, 1, 128), jnp.int32),
            pltpu.SMEM((n, 1, 128), jnp.int32),
            dma((1,)),
            *([dma((n,))] * 8), dma((6,)), dma((6,)), dma((3,)), dma((3,)),
        ],
        compiler_params=pltpu.CompilerParams(
            collective_id=1, has_side_effects=True, vmem_limit_bytes=56 * 2**20
        ),
        name="propagate",
    )(
        pages.reshape(nb, tile, fh),
        band_tiles,
        off_tiles,
        off_row,
        requests,
        label_page.reshape(count // 128, 1, 128),
    )
    return prop_a.reshape(rows, fh), prop_t.reshape(rows, fh), prop_aat.reshape(rows, fh), feats, sel


def per_device(
    pages, band_tiles, off_tiles, off_row, requests, label_page, labels, w_first, w_second
):
    prop_a, prop_t, prop_aat, features, mine = propagated(
        pages, band_tiles, off_tiles, off_row, requests, label_page
    )
    packed = summed_gradients(features, mine, w_first, w_second, labels)
    return handed_out(packed, prop_a, prop_t, prop_aat, w_first, w_second, pages.shape[1])


def solution(mesh):
    placed = (
        P("band", "dp"),
        P("band", None, None, None),
        P("band", None, None),
        P("band"),
        P("band"),
        P("band"),
        P(("band", "dp")),
        P(),
        P(),
    )
    return jax.shard_map(
        per_device,
        mesh=mesh,
        in_specs=placed,
        out_specs=(P("band", "dp"), P("band", "dp"), P("band", "dp"), P(), P()),
        check_vma=False,
    )
```

```python
import functools

import jax
import jax.numpy as jnp
from jax import lax
from jax.experimental import pallas as pl
from jax.experimental.pallas import tpu as pltpu
from jax.sharding import PartitionSpec as P


MESH = pl.DeviceIdType.MESH


def greet(n):
    b, other = lax.axis_index("band"), 1 - lax.axis_index("dp")
    barrier = pltpu.get_barrier_semaphore()
    pl.semaphore_signal(barrier, inc=1, device_id={"dp": other}, device_id_type=MESH)

    def call(d, _):
        pl.semaphore_signal(
            barrier, inc=1, device_id={"band": lax.rem(b + d, n)}, device_id_type=MESH
        )
        return 0

    lax.fori_loop(1, n, call, 0)


def met(n):
    pl.semaphore_wait(pltpu.get_barrier_semaphore(), n)


def remote(src, dst, send_sem, recv_sem, **where):
    return pltpu.make_async_remote_copy(
        src_ref=src, dst_ref=dst, send_sem=send_sem, recv_sem=recv_sem,
        device_id=where, device_id_type=MESH,
    )


def each(start, stop, body):
    def step(d, _):
        body(d)
        return 0

    lax.fori_loop(start, stop, step, 0)


def reduce_kernel(
    g, depth, pieces, by_rows, feats, mine, w1, w2, label, out,
    feat_t, hid, hid_in, err, back, slope, cur, q1s, q1r, q2s, q2r, q3s, q3r,
    s_act, r_act, s_back, r_back, s_one, r_one, s_two, r_two, s_z, r_z,
    s_gz, r_gz, s_g2, r_g2, s_g1, r_g1, s_fw, r_fw,
):
    n = g * g * depth
    b, h = lax.axis_index("band"), lax.axis_index("dp")
    o = 1 - h
    x, y, z = lax.rem(b, g), lax.rem(lax.div(b, g), g), lax.div(b, g * g)
    c1, c2 = x + h * (y - x), y + h * (x - y)
    stride1, stride2 = 1 + h * (g - 1), g - h * (g - 1)
    count, classes = feats.shape[0], w2.shape[1]
    picks, _, fh = mine.shape
    half, width = cur.shape[1:]
    low = hid_in.shape[1]
    top = picks * fh
    quarter = half - top
    low_step = low // pieces
    rows1 = half // g
    rows2 = rows1 // g
    base1 = c1 * rows1
    base2 = base1 + c2 * rows2
    tall, thin = (rows2 // depth, width) if by_rows else (rows2, width // depth)
    f32, bf16, i16 = jnp.float32, jnp.bfloat16, jnp.int16
    fine = 14.0

    def down(start, size):
        return pl.ds(pl.multiple_of(start, 16), size)

    def across(start, size):
        return pl.ds(pl.multiple_of(start, 128), size)

    def member1(d):
        m = lax.rem(c1 + d, g)
        return m, b + (m - c1) * stride1

    def member2(d):
        m = lax.rem(c2 + d, g)
        return m, b + (m - c2) * stride2

    def member_z(d):
        m = lax.rem(z + d, depth)
        return m, b + (m - z) * (g * g)

    def spot_z(m):
        if by_rows:
            return down(base2 + m * tall, tall), pl.ds(0, width)
        return down(base2, rows2), across(m * thin, thin)

    def encode(value, ref):
        rows, cols = value.shape
        most = jnp.max(jnp.abs(value), axis=0, keepdims=True)
        power = jnp.floor(jnp.log2(jnp.maximum(most, 1e-33))) + 1.0
        whole = jnp.round(value * jnp.exp2(fine - power)).astype(jnp.int32)
        ref[:rows] = whole.astype(i16)
        ref[rows:] = jnp.broadcast_to(power, (16, cols)).astype(jnp.int32).astype(i16)

    def decode(ref):
        rows = ref.shape[0] - 16
        power = ref[rows:].astype(jnp.int32).astype(f32)[:1]
        return ref[:rows].astype(jnp.int32).astype(f32) * jnp.exp2(power - fine)

    def act_copies():
        return (
            remote(hid.at[:, across(o * low, low)], hid_in, s_act.at[0], r_act.at[0], dp=o),
            remote(err.at[0], err.at[1], s_act.at[1], r_act.at[1], dp=o),
        )

    def back_copy(p):
        return remote(back.at[p, 0], back.at[p, 1], s_back.at[p], r_back.at[p], dp=o)

    def one(p, d):
        return remote(
            q1s.at[p, d - 1], q1r.at[p, d - 1], s_one.at[p, d - 1], r_one.at[p, d - 1],
            band=member1(d)[1],
        )

    def two(p, d):
        return remote(
            q2s.at[p, d - 1], q2r.at[p, d - 1], s_two.at[p, d - 1], r_two.at[p, d - 1],
            band=member2(d)[1],
        )

    def along_z(p, d):
        return remote(
            q3s.at[p, d - 1], q3r.at[p, d - 1], s_z.at[p, d - 1], r_z.at[p, d - 1],
            band=member_z(d)[1],
        )

    def back_z(p, d, taking=False):
        m, t = member_z(d)
        owner = lax.rem(z + depth - d, depth) if taking else z
        rows, cols = spot_z(owner)
        spot = out.at[h, p, rows, cols]
        return remote(spot, spot, s_gz.at[p, d - 1], r_gz.at[p, d - 1], band=t)

    def back2(p, d, taking=False):
        m, t = member2(d)
        owner = lax.rem(c2 + g - d, g) if taking else c2
        spot = out.at[h, p, down(base1 + owner * rows2, rows2)]
        return remote(spot, spot, s_g2.at[p, d - 1], r_g2.at[p, d - 1], band=t)

    def back1(p, d, taking=False):
        m, t = member1(d)
        owner = lax.rem(c1 + g - d, g) if taking else c1
        spot = out.at[h, p, down(owner * rows1, rows1)]
        return remote(spot, spot, s_g1.at[p, d - 1], r_g1.at[p, d - 1], band=t)

    def forward(p, core):
        spot = out.at[core, p]
        return remote(spot, spot, s_fw.at[p], r_fw.at[p], dp=o)

    def dot(lhs, rhs, i, j):
        return lax.dot_general(lhs, rhs, (((i,), (j,)), ((), ())), preferred_element_type=f32)

    def errors_back(p):
        w = slice(p * width, (p + 1) * width)
        signal = dot(err[0], w2[w], 1, 1) * slope[:, w]
        back[p, 0] = signal.astype(bf16)
        back_copy(p).start()

    def gradients(p):
        back_copy(p).wait_recv()
        cur[p, :top] = dot(feat_t[...], back[p].reshape(2 * count, width), 1, 0)
        if p == 0:
            for copy in act_copies():
                copy.wait_recv()
        for j in range(low_step // quarter):
            start = p * low_step + j * quarter
            cur[p, top:, j * classes : (j + 1) * classes] = dot(
                hid[:, across(h * low + start, quarter)], err[0], 0, 0
            ) + dot(hid_in[:, start : start + quarter], err[1], 0, 0)
        for d in range(1, g):
            encode(cur[p, down(member1(d)[0] * rows1, rows1)], q1s.at[p, d - 1])
            one(p, d).start()

    def after_one(p):
        for d in range(1, g):
            one(p, d).wait_recv()
            cur[p, down(base1, rows1)] += decode(q1r.at[p, d - 1])
        for d in range(1, g):
            encode(cur[p, down(base1 + member2(d)[0] * rows2, rows2)], q2s.at[p, d - 1])
            two(p, d).start()

    def after_two(p):
        for d in range(1, g):
            two(p, d).wait_recv()
            cur[p, down(base2, rows2)] += decode(q2r.at[p, d - 1])
        for d in range(1, depth):
            rows, cols = spot_z(member_z(d)[0])
            encode(cur[p, rows, cols], q3s.at[p, d - 1])
            along_z(p, d).start()

    def after_z(p):
        rows, cols = spot_z(z)
        total = cur[p, rows, cols]
        for d in range(1, depth):
            along_z(p, d).wait_recv()
            total += decode(q3r.at[p, d - 1])
        out[h, p, rows, cols] = total.astype(bf16)
        for d in range(1, depth):
            back_z(p, d).start()

    def after_back_z(p):
        for d in range(1, depth):
            back_z(p, d, True).wait_recv()
        for d in range(1, g):
            back2(p, d).start()

    def after_back2(p):
        for d in range(1, g):
            back2(p, d, True).wait_recv()
        for d in range(1, g):
            back1(p, d).start()

    def after_back1(p):
        for d in range(1, g):
            back1(p, d, True).wait_recv()
        forward(p, h).start()

    span = label.shape[2]
    lane = lax.broadcasted_iota(jnp.int32, (span, span), 1)
    greet(n)
    step = min(width, 256)
    for c in range(hid.shape[1] // step):
        w = slice(c * step, (c + 1) * step)
        pre = dot(feats[...], w1[:, w], 1, 0)
        sigma = jax.nn.sigmoid(pre)
        hid[:, w] = (pre * sigma).astype(bf16)
        slope[:, w] = sigma * (1.0 + pre * (1.0 - sigma))
    for i in range(count // span):
        rows = slice(i * span, (i + 1) * span)
        logits = dot(hid[rows], w2[...], 1, 0)
        powers = jnp.exp(logits - jnp.max(logits, axis=-1, keepdims=True))
        shares = powers / jnp.sum(powers, axis=-1, keepdims=True)
        wanted = jnp.broadcast_to(label[i], (span, span)).T
        label_hot = jnp.concatenate(
            [jnp.where(wanted == lane + c * span, 1.0, 0.0) for c in range(classes // span)], axis=1
        )
        err[0, rows] = ((shares - label_hot) / (2 * count)).astype(bf16)
    met(n)
    for copy in act_copies():
        copy.start()
    for j in range(picks):
        own = feats[:, across((2 * j + h) * fh, fh)]
        feat_t[j * fh : (j + 1) * fh, :count] = own.T
        feat_t[j * fh : (j + 1) * fh, count:] = mine[j].T
    stages = (
        errors_back, gradients, after_one, after_two, after_z, after_back_z, after_back2, after_back1
    )
    for t in range(len(stages) + pieces - 1):
        for p in reversed(range(pieces)):
            if 0 <= t - p < len(stages):
                stages[t - p](p)
    for copy in act_copies():
        copy.wait_send()
    for p in range(pieces):
        back_copy(p).wait_send()
        for d in range(1, g):
            for copy in (one(p, d), two(p, d), back2(p, d), back1(p, d)):
                copy.wait_send()
        for d in range(1, depth):
            along_z(p, d).wait_send()
            back_z(p, d).wait_send()
        forward(p, h).wait_send()
        forward(p, o).wait_recv()


def hand_out(top, fh, packed, a, t, aat, out_a, out_t, out_aat, grad1, grad2, sem):
    _, pieces, half, width = packed.shape
    classes = grad2.shape[1]
    quarter = half - top
    groups = width // classes
    copies = [
        pltpu.make_async_copy(source, target, sem.at[i])
        for i, (source, target) in enumerate(((a, out_a), (t, out_t), (aat, out_aat)))
    ]
    for core in range(2):
        for p in range(pieces):
            for j in range(top // fh):
                copies.append(
                    pltpu.make_async_copy(
                        packed.at[core, p, pl.ds(j * fh, fh)],
                        grad1.at[pl.ds((2 * j + core) * fh, fh), pl.ds(p * width, width)],
                        sem.at[len(copies)],
                    )
                )
            for j in range(groups):
                start = ((core * pieces + p) * groups + j) * quarter
                copies.append(
                    pltpu.make_async_copy(
                        packed.at[core, p, pl.ds(top, quarter), pl.ds(j * classes, classes)],
                        grad2.at[pl.ds(start, quarter)],
                        sem.at[len(copies)],
                    )
                )
    for copy in copies:
        copy.start()
    for copy in copies:
        copy.wait()


def summed_gradients(features, mine, w_first, w_second, labels):
    n = lax.axis_size("band")
    g = max(1, round((n / 2) ** (1 / 3)))
    if n % (g * g):
        g = 1
    depth = n // (g * g)
    hid, classes = w_second.shape
    picks, count, fh = mine.shape
    top, low = picks * fh, hid // 2
    half = (w_first.size + w_second.size) // (2 * hid)
    rows2 = half // (g * g)
    by_rows = rows2 % (16 * depth) == 0
    pieces = max(1, hid // 256 if by_rows else hid // (128 * depth))
    width = hid // pieces
    f32, bf16, i16 = jnp.float32, jnp.bfloat16, jnp.int16
    tall, thin = (rows2 // depth, width) if by_rows else (rows2, width // depth)
    vmem = pl.BlockSpec(memory_space=pltpu.VMEM)
    dma = pltpu.SemaphoreType.DMA
    side, deep = max(1, g - 1), max(1, depth - 1)
    near, far = dma((pieces, side)), dma((pieces, deep))
    first = pltpu.VMEM((pieces, side, half // g + 16, width), i16)
    second = pltpu.VMEM((pieces, side, rows2 + 16, width), i16)
    third = pltpu.VMEM((pieces, deep, tall + 16, thin), i16)
    return pl.pallas_call(
        functools.partial(reduce_kernel, g, depth, pieces, by_rows),
        out_shape=jax.ShapeDtypeStruct((2, pieces, half, width), bf16),
        in_specs=[vmem] * 5,
        out_specs=vmem,
        scratch_shapes=[
            pltpu.VMEM((top, 2 * count), bf16),
            pltpu.VMEM((count, hid), bf16),
            pltpu.VMEM((count, low), bf16),
            pltpu.VMEM((2, count, classes), bf16),
            pltpu.VMEM((pieces, 2, count, width), bf16),
            pltpu.VMEM((count, hid), f32),
            pltpu.VMEM((pieces, half, width), f32),
            first, first, second, second, third, third,
            dma((2,)), dma((2,)), dma((pieces,)), dma((pieces,)),
            near, near, near, near, far, far, far, far, near, near, near, near,
            dma((pieces,)), dma((pieces,)),
        ],
        compiler_params=pltpu.CompilerParams(
            collective_id=0, has_side_effects=True, vmem_limit_bytes=40 * 2**20
        ),
        name="grad_sum",
    )(features, mine, w_first, w_second, labels.reshape(count // 128, 1, 128))


def handed_out(packed, prop_a, prop_t, prop_aat, w_first, w_second, fh):
    top = w_first.shape[0] // 2
    _, pieces, half, width = packed.shape
    groups = width // w_second.shape[1]
    total = 3 + 2 * pieces * (top // fh + groups)
    vmem = pl.BlockSpec(memory_space=pltpu.VMEM)
    anywhere = pl.BlockSpec(memory_space=pl.ANY)
    return pl.pallas_call(
        functools.partial(hand_out, top, fh),
        out_shape=tuple(
            jax.ShapeDtypeStruct(a.shape, a.dtype)
            for a in (prop_a, prop_t, prop_aat, w_first, w_second)
        ),
        in_specs=[vmem] * 4,
        out_specs=(anywhere,) * 5,
        scratch_shapes=[pltpu.SemaphoreType.DMA((total,))],
        name="hand_out",
    )(packed, prop_a, prop_t, prop_aat)


def propagate_kernel(
    n, pages, tiles, offs, off_row, req, label, prop_a, prop_t, prop_aat, feats, sel,
    hot, back_send, back_land, page_send, page_land, t_send, t_land, pad, padt,
    rim_send, rim_land, inner, acc, req_out, req_land, served, local_sem,
    s_req, r_req, s_back, r_back, s_page, r_page, s_t, r_t, s_edge, r_edge, s_pick, r_pick,
):
    b, h = lax.axis_index("band"), lax.axis_index("dp")
    o = 1 - h
    nb, tile, fh = pages.shape
    left, right = lax.rem(b + n - 1, n), lax.rem(b + 1, n)
    half = feats.shape[0]
    f32, bf16 = jnp.float32, jnp.bfloat16

    def ahead(d):
        return lax.rem(b + d, n)

    def behind(d):
        return lax.rem(b + n - d, n)

    def tdot(x, y):
        return lax.dot_general(x, y, (((0,), (0,)), ((), ())), preferred_element_type=f32)

    def dot(x, y):
        return jnp.dot(x, y, preferred_element_type=f32)

    barrier = pltpu.get_barrier_semaphore()
    pl.semaphore_signal(barrier, inc=1, device_id={"dp": o}, device_id_type=MESH)
    each(
        1,
        n,
        lambda d: pl.semaphore_signal(
            barrier, inc=1, device_id={"band": ahead(d)}, device_id_type=MESH
        ),
    )
    chunk = label.shape[2]
    lane = lax.broadcasted_iota(jnp.int32, (chunk, chunk), 1)

    def build_hot(i):
        rows = pl.ds(pl.multiple_of(i * chunk, chunk), chunk)
        wanted = jnp.broadcast_to(label[i], (chunk, chunk)).T
        for c in range(nb * tile // chunk):
            hot[rows, c * chunk : (c + 1) * chunk] = jnp.where(
                wanted == lane + c * chunk, 1.0, 0.0
            ).astype(bf16)

    def build_req(t):
        req_out[t] = jnp.full((1, 128), req[t], jnp.int32)

    each(0, n, build_req)
    each(0, hot.shape[0] // chunk, build_hot)
    rim_send[0] = tdot(tiles[0, 0], pages[0])
    rim_send[1] = tdot(tiles[nb - 1, 2], pages[nb - 1])
    pl.semaphore_wait(barrier, n)

    def ask(d):
        t = ahead(d)
        return remote(req_out.at[t], req_land.at[d], s_req.at[d], r_req.at[d], band=t)

    def send_back(d):
        return remote(back_send.at[d], back_land.at[d], s_back.at[d], r_back.at[d], band=ahead(d))

    def send_page(d):
        return remote(page_send.at[d], page_land.at[d], s_page.at[d], r_page.at[d], band=behind(d))

    def send_t(d):
        return remote(t_send.at[d], t_land.at[d], s_t.at[d], r_t.at[d], band=behind(d))

    def edges(source, field, i):
        first, last = source
        return (
            remote(first, field.at[nb + 1], s_edge.at[i], r_edge.at[i], band=left),
            remote(last, field.at[0], s_edge.at[i + 1], r_edge.at[i + 1], band=right),
        )

    each(1, n, lambda d: ask(d).start())
    rims = (
        remote(rim_send.at[0], rim_land.at[0], s_edge.at[2], r_edge.at[2], band=left),
        remote(rim_send.at[1], rim_land.at[1], s_edge.at[3], r_edge.at[3], band=right),
    )
    page_edges = edges((pages.at[0], pages.at[nb - 1]), pad, 0)
    for copy in rims + page_edges:
        copy.start()

    def back_term(d):
        k = ahead(d)
        return tdot(offs[k], pages[off_row[k]]).astype(bf16)

    def make_back(d):
        back_send[d] = back_term(d)
        send_back(d).start()

    each(1, n, make_back)
    back_land[0] = back_term(0)
    req_land[0] = req_out[b]
    each(1, n, lambda d: ask(d).wait_recv())
    to_scalar = pltpu.make_async_copy(req_land, served, local_sem.at[0])
    to_scalar.start()
    to_scalar.wait()

    def make_page(d):
        page_send[d] = pages[served[d, 0, 0]]
        send_page(d).start()

    each(1, n, make_page)
    page_land[0] = pages[served[0, 0, 0]]

    inner[0] = tdot(tiles[0, 1], pages[0]) + tdot(tiles[1, 0], pages[1])
    inner[nb - 1] = tdot(tiles[nb - 1, 1], pages[nb - 1]) + tdot(tiles[nb - 2, 2], pages[nb - 2])

    def adjoint(m):
        inner[m] = (
            tdot(tiles[m - 1, 2], pages[m - 1])
            + tdot(tiles[m, 1], pages[m])
            + tdot(tiles[m + 1, 0], pages[m + 1])
        )

    each(1, nb - 1, adjoint)
    for copy in rims:
        copy.wait()
    inner[nb - 1] += jnp.where(b < n - 1, 1.0, 0.0) * rim_land[0]
    inner[0] += jnp.where(b > 0, 1.0, 0.0) * rim_land[1]

    def spread_rows(target, spot, term):
        for r in range(nb):
            target[r] += jnp.where(spot == r, 1.0, 0.0) * term

    def take_back(d):
        spread_rows(inner, served[d, 0, 0], back_land[d].astype(f32))

    take_back(0)

    def await_back(d):
        send_back(d).wait_recv()
        take_back(d)

    each(1, n, await_back)

    def round_t(r):
        block = inner[r].astype(bf16)
        padt[r + 1] = block
        prop_t[r] = block

    each(0, nb, round_t)
    t_edges = edges((padt.at[1], padt.at[nb]), padt, 4)
    for copy in t_edges:
        copy.start()

    def make_t(d):
        t_send[d] = prop_t[served[d, 0, 0]]
        send_t(d).start()

    each(1, n, make_t)
    t_land[0] = prop_t[served[0, 0, 0]]

    def copy_pages(r):
        pad[r + 1] = pages[r]

    each(0, nb, copy_pages)

    def clear_ends(field):
        @pl.when(b == 0)
        def _():
            field[0] = jnp.zeros((tile, fh), bf16)

        @pl.when(b == n - 1)
        def _():
            field[nb + 1] = jnp.zeros((tile, fh), bf16)

    def near(field):
        def row(r):
            weights = jnp.concatenate([tiles[r, 0], tiles[r, 1], tiles[r, 2]], axis=1)
            window = jnp.concatenate([field[r], field[r + 1], field[r + 2]], axis=0)
            acc[r] = dot(weights, window)

        each(0, nb, row)

    def take_off(land, d):
        k = ahead(d)
        spread_rows(acc, off_row[k], dot(offs[k], land[d]))

    def pick(j, field):
        whole = field[1 : nb + 1].reshape(nb * tile, fh)
        step = half // 2

        def rows_of(core, c):
            return pl.ds(pl.multiple_of(core * half + c * step, step), step)

        columns = pl.ds(pl.multiple_of((2 * j + h) * fh, fh), fh)
        for c in range(2):
            sel[j, c * step : (c + 1) * step] = dot(hot[rows_of(o, c)], whole).astype(bf16)
        give = remote(sel.at[j], feats.at[:, columns], s_pick.at[j], r_pick.at[j], dp=o)
        give.start()
        for c in range(2):
            feats[c * step : (c + 1) * step, columns] = dot(hot[rows_of(h, c)], whole).astype(bf16)
        return give

    gives = [pick(1, padt)]
    for copy in page_edges:
        copy.wait()
    clear_ends(pad)
    near(pad)
    take_off(page_land, 0)

    def await_page(d):
        send_page(d).wait_recv()
        take_off(page_land, d)

    each(1, n, await_page)

    def round_a(r):
        block = acc[r].astype(bf16)
        pad[r + 1] = block
        prop_a[r] = block

    each(0, nb, round_a)
    gives.append(pick(0, pad))
    for copy in t_edges:
        copy.wait()
    clear_ends(padt)
    near(padt)
    take_off(t_land, 0)

    def await_t(d):
        send_t(d).wait_recv()
        take_off(t_land, d)

    each(1, n, await_t)

    def round_aat(r):
        block = acc[r].astype(bf16)
        padt[r + 1] = block
        prop_aat[r] = block

    each(0, nb, round_aat)
    gives.append(pick(2, padt))

    def finish(d):
        ask(d).wait_send()
        send_back(d).wait_send()
        send_page(d).wait_send()
        send_t(d).wait_send()

    each(1, n, finish)
    for j, give in zip((1, 0, 2), gives):
        give.wait_send()
        columns = pl.ds(pl.multiple_of((2 * j + o) * fh, fh), fh)
        remote(
            sel.at[j], feats.at[:, columns], s_pick.at[j], r_pick.at[j], dp=o
        ).wait_recv()


def propagated(pages, band_tiles, off_tiles, off_row, requests, label_page):
    n = lax.axis_size("band")
    tile = band_tiles.shape[-1]
    rows, fh = pages.shape
    nb = rows // tile
    count = label_page.shape[0]
    bf16, f32 = jnp.bfloat16, jnp.float32
    vmem = pl.BlockSpec(memory_space=pltpu.VMEM)
    smem = pl.BlockSpec(memory_space=pltpu.SMEM)
    dma = pltpu.SemaphoreType.DMA
    blocks = jax.ShapeDtypeStruct((nb, tile, fh), bf16)
    per_band = pltpu.VMEM((n, tile, fh), bf16)
    padded = pltpu.VMEM((nb + 2, tile, fh), bf16)
    half = count // 2
    prop_a, prop_t, prop_aat, feats, sel = pl.pallas_call(
        functools.partial(propagate_kernel, n),
        out_shape=(
            blocks, blocks, blocks,
            jax.ShapeDtypeStruct((half, 6 * fh), bf16),
            jax.ShapeDtypeStruct((3, half, fh), bf16),
        ),
        in_specs=[vmem, vmem, vmem, smem, smem, vmem],
        out_specs=(vmem,) * 5,
        scratch_shapes=[
            pltpu.VMEM((count, rows), bf16),
            per_band, per_band, per_band, per_band, per_band, per_band,
            padded, padded,
            pltpu.VMEM((2, tile, fh), f32),
            pltpu.VMEM((2, tile, fh), f32),
            pltpu.VMEM((nb, tile, fh), f32),
            pltpu.VMEM((nb, tile, fh), f32),
            pltpu.VMEM((n, 1, 128), jnp.int32),
            pltpu.VMEM((n, 1, 128), jnp.int32),
            pltpu.SMEM((n, 1, 128), jnp.int32),
            dma((1,)),
            *([dma((n,))] * 8), dma((6,)), dma((6,)), dma((3,)), dma((3,)),
        ],
        compiler_params=pltpu.CompilerParams(
            collective_id=1, has_side_effects=True, vmem_limit_bytes=56 * 2**20
        ),
        name="propagate",
    )(
        pages.reshape(nb, tile, fh),
        band_tiles,
        off_tiles,
        off_row,
        requests,
        label_page.reshape(count // 128, 1, 128),
    )
    return prop_a.reshape(rows, fh), prop_t.reshape(rows, fh), prop_aat.reshape(rows, fh), feats, sel


def per_device(
    pages, band_tiles, off_tiles, off_row, requests, label_page, labels, w_first, w_second
):
    prop_a, prop_t, prop_aat, features, mine = propagated(
        pages, band_tiles, off_tiles, off_row, requests, label_page
    )
    packed = summed_gradients(features, mine, w_first, w_second, labels)
    return handed_out(packed, prop_a, prop_t, prop_aat, w_first, w_second, pages.shape[1])


def solution(mesh):
    placed = (
        P("band", "dp"),
        P("band", None, None, None),
        P("band", None, None),
        P("band"),
        P("band"),
        P("band"),
        P(("band", "dp")),
        P(),
        P(),
    )
    return jax.shard_map(
        per_device,
        mesh=mesh,
        in_specs=placed,
        out_specs=(P("band", "dp"), P("band", "dp"), P("band", "dp"), P(), P()),
        check_vma=False,
    )
```

```python
import functools

import jax
import jax.numpy as jnp
from jax import lax
from jax.experimental import pallas as pl
from jax.experimental.pallas import tpu as pltpu
from jax.sharding import PartitionSpec as P


MESH = pl.DeviceIdType.MESH
PACE = 3.2
SPLIT = 2


def greet(n):
    b, other = lax.axis_index("band"), 1 - lax.axis_index("dp")
    barrier = pltpu.get_barrier_semaphore()
    pl.semaphore_signal(barrier, inc=1, device_id={"dp": other}, device_id_type=MESH)

    def call(d, _):
        pl.semaphore_signal(
            barrier, inc=1, device_id={"band": lax.rem(b + d, n)}, device_id_type=MESH
        )
        return 0

    lax.fori_loop(1, n, call, 0)


def met(n):
    pl.semaphore_wait(pltpu.get_barrier_semaphore(), n)


def remote(src, dst, send_sem, recv_sem, **where):
    return pltpu.make_async_remote_copy(
        src_ref=src, dst_ref=dst, send_sem=send_sem, recv_sem=recv_sem,
        device_id=where, device_id_type=MESH,
    )


def each(start, stop, body):
    def step(d, _):
        body(d)
        return 0

    lax.fori_loop(start, stop, step, 0)


def by(step, stop, body):
    if stop % step:
        return each(0, stop, body)

    def several(i):
        for j in range(step):
            body(i * step + j)

    each(0, stop // step, several)


def training(
    g, depth, split, by_rows, feats, mine, w1, w2, label, grad1, grad2, out,
    feat_t, hid, hid_in, err, back, slope, cur, q1s, q1r, q2s, q2r, q3s, q3r, p3s, p3r,
    s_act, r_act, s_back, r_back, s_one, r_one, s_two, r_two, s_z, r_z, s_pz, r_pz,
    s_gz, r_gz, s_g2, r_g2, s_g1, r_g1, s_fw, r_fw, s_out,
):
    n = g * g * depth
    b, h = lax.axis_index("band"), lax.axis_index("dp")
    o = 1 - h
    x, y, z = lax.rem(b, g), lax.rem(lax.div(b, g), g), lax.div(b, g * g)
    c1, c2 = x + h * (y - x), y + h * (x - y)
    stride1, stride2 = 1 + h * (g - 1), g - h * (g - 1)
    count, classes = feats.shape[0], w2.shape[1]
    picks, _, fh = mine.shape
    chunks, half, broad = cur.shape
    pieces, width = chunks * split, broad // split
    low = hid_in.shape[1]
    top = picks * fh
    quarter = half - top
    low_step = low // chunks
    rows1 = half // g
    rows2 = rows1 // g
    base1 = c1 * rows1
    base2 = base1 + c2 * rows2
    tall, thin = (rows2 // depth, width) if by_rows else (rows2, width // depth)
    f32, bf16, i16 = jnp.float32, jnp.bfloat16, jnp.int16
    fine = 14.0

    def down(start, size):
        return pl.ds(pl.multiple_of(start, 16), size)

    def across(start, size):
        return pl.ds(pl.multiple_of(start, 128), size)

    def member1(d):
        m = lax.rem(c1 + d, g)
        return m, b + (m - c1) * stride1

    def member2(d):
        m = lax.rem(c2 + d, g)
        return m, b + (m - c2) * stride2

    def member_z(d):
        m = lax.rem(z + d, depth)
        return m, b + (m - z) * (g * g)

    def wide(p):
        return pl.ds(p % split * width, width)

    def spot_z(p, m):
        if by_rows:
            return down(base2 + m * tall, tall), wide(p)
        return down(base2, rows2), across(p % split * width + m * thin, thin)

    def encode(value, ref, scale=None):
        rows, cols = value.shape
        most = jnp.max(jnp.abs(value), axis=0, keepdims=True)
        power = jnp.floor(jnp.log2(jnp.maximum(most, 1e-33))) + 1.0
        whole = jnp.round(value * jnp.exp2(fine - power)).astype(jnp.int32)
        ref[:rows] = whole.astype(i16)
        if scale is None:
            ref[rows:] = jnp.broadcast_to(power, (16, cols)).astype(jnp.int32).astype(i16)
        else:
            scale[...] = power

    def decode(ref, scale=None):
        if scale is not None:
            return ref[...].astype(jnp.int32).astype(f32) * jnp.exp2(scale[...] - fine)
        rows = ref.shape[0] - 16
        power = ref[rows:].astype(jnp.int32).astype(f32)[:1]
        return ref[:rows].astype(jnp.int32).astype(f32) * jnp.exp2(power - fine)

    def hidden_copy():
        return remote(hid.at[:, across(o * low, low)], hid_in, s_act.at[0], r_act.at[0], dp=o)

    def error_copy():
        return remote(err.at[0], err.at[1], s_act.at[1], r_act.at[1], dp=o)

    def back_copy(p):
        return remote(back.at[p, 0], back.at[p, 1], s_back.at[p], r_back.at[p], dp=o)

    def one(p, d):
        return remote(
            q1s.at[p, d - 1], q1r.at[p, d - 1], s_one.at[p, d - 1], r_one.at[p, d - 1],
            band=member1(d)[1],
        )

    def two(p, d):
        return remote(
            q2s.at[p, d - 1], q2r.at[p, d - 1], s_two.at[p, d - 1], r_two.at[p, d - 1],
            band=member2(d)[1],
        )

    def along_z(p, d):
        return remote(
            q3s.at[p, d - 1], q3r.at[p, d - 1], s_z.at[p, d - 1], r_z.at[p, d - 1],
            band=member_z(d)[1],
        )

    def power_z(p, d):
        return remote(
            p3s.at[p, d - 1], p3r.at[p, d - 1], s_pz.at[p, d - 1], r_pz.at[p, d - 1],
            band=member_z(d)[1],
        )

    def back_z(p, d, taking=False):
        m, t = member_z(d)
        owner = lax.rem(z + depth - d, depth) if taking else z
        rows, cols = spot_z(p, owner)
        spot = out.at[h, p // split, rows, cols]
        return remote(spot, spot, s_gz.at[p, d - 1], r_gz.at[p, d - 1], band=t)

    def back2(p, d, taking=False):
        m, t = member2(d)
        owner = lax.rem(c2 + g - d, g) if taking else c2
        spot = out.at[h, p // split, down(base1 + owner * rows2, rows2), wide(p)]
        return remote(spot, spot, s_g2.at[p, d - 1], r_g2.at[p, d - 1], band=t)

    def back1(p, d, taking=False):
        m, t = member1(d)
        owner = lax.rem(c1 + g - d, g) if taking else c1
        spot = out.at[h, p // split, down(owner * rows1, rows1), wide(p)]
        return remote(spot, spot, s_g1.at[p, d - 1], r_g1.at[p, d - 1], band=t)

    def forward(p, core):
        spot = out.at[core, p // split, :, wide(p)]
        return remote(spot, spot, s_fw.at[p], r_fw.at[p], dp=o)

    def dot(lhs, rhs, i, j):
        return lax.dot_general(lhs, rhs, (((i,), (j,)), ((), ())), preferred_element_type=f32)

    def writes(core, q):
        target = pl.ds(q * broad, broad)
        copies = [
            pltpu.make_async_copy(
                out.at[core, q, pl.ds(j * fh, fh)],
                grad1.at[across((2 * j + core) * fh, fh), target],
                s_out.at[core, q, j],
            )
            for j in range(picks)
        ]
        for j in range(low_step // quarter):
            start = core * low + q * low_step + j * quarter
            copies.append(
                pltpu.make_async_copy(
                    out.at[core, q, pl.ds(top, quarter), pl.ds(j * classes, classes)],
                    grad2.at[down(start, quarter)],
                    s_out.at[core, q, picks + j],
                )
            )
        return copies

    def errors_back(q):
        w = slice(q * broad, (q + 1) * broad)
        signal = dot(err[0], w2[w], 1, 1) * slope[:, w]
        back[q, 0] = signal.astype(bf16)
        back_copy(q).start()

    def gradients(q):
        back_copy(q).wait_recv()
        cur[q, :top] = dot(feat_t[...], back[q].reshape(2 * count, broad), 1, 0)
        if q == 0:
            for copy in (hidden_copy(), error_copy()):
                copy.wait_recv()
        for j in range(low_step // quarter):
            start = q * low_step + j * quarter
            cur[q, top:, j * classes : (j + 1) * classes] = dot(
                hid[:, across(h * low + start, quarter)], err[0], 0, 0
            ) + dot(hid_in[:, start : start + quarter], err[1], 0, 0)
        for p in range(q * split, (q + 1) * split):
            for d in range(1, g):
                rows = down(member1(d)[0] * rows1, rows1)
                encode(cur[q, rows, wide(p)], q1s.at[p, d - 1])
                one(p, d).start()

    def after_one(p):
        q = p // split
        for d in range(1, g):
            one(p, d).wait_recv()
            cur[q, down(base1, rows1), wide(p)] += decode(q1r.at[p, d - 1])
        for d in range(1, g):
            rows = down(base1 + member2(d)[0] * rows2, rows2)
            encode(cur[q, rows, wide(p)], q2s.at[p, d - 1])
            two(p, d).start()

    def after_two(p):
        q = p // split
        for d in range(1, g):
            two(p, d).wait_recv()
            cur[q, down(base2, rows2), wide(p)] += decode(q2r.at[p, d - 1])
        for d in range(1, depth):
            rows, cols = spot_z(p, member_z(d)[0])
            encode(cur[q, rows, cols], q3s.at[p, d - 1], p3s.at[p, d - 1])
            along_z(p, d).start()
            power_z(p, d).start()

    def after_z(p):
        rows, cols = spot_z(p, z)
        total = cur[p // split, rows, cols]
        for d in range(1, depth):
            along_z(p, d).wait_recv()
            power_z(p, d).wait_recv()
            total += decode(q3r.at[p, d - 1], p3r.at[p, d - 1])
        out[h, p // split, rows, cols] = total.astype(bf16)
        for d in range(1, depth):
            back_z(p, d).start()

    def after_back_z(p):
        for d in range(1, depth):
            back_z(p, d, True).wait_recv()
        for d in range(1, g):
            back2(p, d).start()

    def after_back2(p):
        for d in range(1, g):
            back2(p, d, True).wait_recv()
        for d in range(1, g):
            back1(p, d).start()

    def after_back1(p):
        for d in range(1, g):
            back1(p, d, True).wait_recv()
        forward(p, h).start()
        if (p + 1) % split == 0:
            for copy in writes(h, p // split):
                copy.start()

    def after_forward(p):
        forward(p, o).wait_recv()
        if (p + 1) % split == 0:
            for copy in writes(o, p // split):
                copy.start()

    span = label.shape[2]
    lane = lax.broadcasted_iota(jnp.int32, (span, span), 1)
    step = min(broad, 256)
    parts = [slice(c * step, (c + 1) * step) for c in range(hid.shape[1] // step)]
    known = 2 * (picks - 1) * fh

    def turn(j):
        feat_t[j * fh : (j + 1) * fh, :count] = feats[:, across((2 * j + h) * fh, fh)].T
        feat_t[j * fh : (j + 1) * fh, count:] = mine[j].T

    def early():
        for w in parts:
            slope[:, w] = dot(feats[:, :known], w1[:known, w], 1, 0)
        for j in range(picks - 1):
            turn(j)

    def forward_pass():
        for w in parts:
            pre = slope[:, w] + dot(feats[:, known:], w1[known:, w], 1, 0)
            sigma = jax.nn.sigmoid(pre)
            hid[:, w] = (pre * sigma).astype(bf16)
            slope[:, w] = sigma * (1.0 + pre * (1.0 - sigma))
        hidden_copy().start()
        for i in range(count // span):
            rows = slice(i * span, (i + 1) * span)
            logits = dot(hid[rows], w2[...], 1, 0)
            powers = jnp.exp(logits - jnp.max(logits, axis=-1, keepdims=True))
            shares = powers / jnp.sum(powers, axis=-1, keepdims=True)
            wanted = jnp.broadcast_to(label[i], (span, span)).T
            label_hot = jnp.concatenate(
                [jnp.where(wanted == lane + c * span, 1.0, 0.0) for c in range(classes // span)],
                axis=1,
            )
            err[0, rows] = ((shares - label_hot) / (2 * count)).astype(bf16)
        error_copy().start()

    def late():
        forward_pass()
        turn(picks - 1)
        stages = (
            after_one, after_two, after_z, after_back_z, after_back2, after_back1, after_forward
        )
        plan = []
        for q in range(chunks):
            plan.append((q * split * 1.0, errors_back, q))
            plan.append((q * split + PACE, gradients, q))
        for p in range(pieces):
            for i, stage in enumerate(stages):
                plan.append((p + (i + 2) * PACE, stage, p))
        plan.sort(key=lambda item: item[0])
        for _, stage, p in plan:
            stage(p)
        for copy in (hidden_copy(), error_copy()):
            copy.wait_send()
        for q in range(chunks):
            back_copy(q).wait_send()
            for core in range(2):
                for copy in writes(core, q):
                    copy.wait()
        for p in range(pieces):
            for d in range(1, g):
                for copy in (one(p, d), two(p, d), back2(p, d), back1(p, d)):
                    copy.wait_send()
            for d in range(1, depth):
                along_z(p, d).wait_send()
                power_z(p, d).wait_send()
                back_z(p, d).wait_send()
            forward(p, h).wait_send()

    return early, late


def propagate(
    n, pages_at, tiles_at, offs_at, w1_at, w2_at, off_row, req, label,
    out_a, out_t, out_aat, prop_a, prop_t, prop_aat, pages, tiles, offs, w1, w2, feats, sel, hot, links,
    back_send, back_land, page_send, page_land, t_land, pad, padt,
    rim_send, rim_land, inner, acc, req_out, req_land, served, off_key, off_prev, off_last, ask_key, ask_prev, ask_last, load_sem, local_sem,
    s_req, r_req, s_back, r_back, s_page, r_page, s_t, r_t, s_edge, r_edge, s_pick, r_pick,
    early,
):
    b, h = lax.axis_index("band"), lax.axis_index("dp")
    o = 1 - h
    nb, tile, fh = pages.shape
    left, right = lax.rem(b + n - 1, n), lax.rem(b + 1, n)
    half = feats.shape[0]
    f32, bf16 = jnp.float32, jnp.bfloat16
    batch = 4 if n % 4 == 0 else 1

    def ahead(d):
        return lax.rem(b + d, n)

    def behind(d):
        return lax.rem(b + n - d, n)

    def tdot(x, y):
        return lax.dot_general(x, y, (((0,), (0,)), ((), ())), preferred_element_type=f32)

    def dot(x, y):
        return jnp.dot(x, y, preferred_element_type=f32)

    loads = [
        pltpu.make_async_copy(source, target, load_sem.at[i])
        for i, (source, target) in enumerate(
            ((pages_at, pages), (offs_at, offs), (tiles_at, tiles), (w1_at, w1), (w2_at, w2))
        )
    ]
    stores = [
        pltpu.make_async_copy(source, target, load_sem.at[len(loads) + i])
        for i, (source, target) in enumerate(((prop_a, out_a), (prop_t, out_t), (prop_aat, out_aat)))
    ]
    greet(n)
    for load in loads:
        load.start()

    def ask(d):
        t = ahead(d)
        return remote(req_out.at[t], req_land.at[d], s_req.at[d], r_req.at[d], band=t)

    def send_back(d):
        return remote(back_send.at[d], back_land.at[d], s_back.at[d], r_back.at[d], band=ahead(d))

    def send_page(d):
        return remote(page_send.at[d], page_land.at[d], s_page.at[d], r_page.at[d], band=behind(d))

    def send_t(d):
        return remote(back_send.at[d], t_land.at[d], s_t.at[d], r_t.at[d], band=behind(d))

    def edges(source, field, i):
        first, last = source
        return (
            remote(first, field.at[nb + 1], s_edge.at[i], r_edge.at[i], band=left),
            remote(last, field.at[0], s_edge.at[i + 1], r_edge.at[i + 1], band=right),
        )

    def build_req(t):
        req_out[t] = jnp.full((1, 128), req[t], jnp.int32)

    each(0, n, build_req)
    loads[0].wait()
    loads[1].wait()

    def make_back(d):
        k = ahead(d)
        back_send[d] = tdot(offs[k], pages[off_row[k]]).astype(bf16)

    by(4, n, make_back)
    met(n)
    each(1, n, lambda d: ask(d).start())
    each(1, n, lambda d: send_back(d).start())
    back_land[0] = back_send[0]
    req_land[0] = req_out[b]
    page_edges = edges((pages.at[0], pages.at[nb - 1]), pad, 0)
    for copy in page_edges:
        copy.start()
    loads[2].wait()
    rim_send[0] = tdot(tiles[0, 0], pages[0])
    rim_send[1] = tdot(tiles[nb - 1, 2], pages[nb - 1])
    rims = (
        remote(rim_send.at[0], rim_land.at[0], s_edge.at[2], r_edge.at[2], band=left),
        remote(rim_send.at[1], rim_land.at[1], s_edge.at[3], r_edge.at[3], band=right),
    )
    for copy in rims:
        copy.start()
    each(1, n, lambda d: ask(d).wait_recv())
    to_scalar = pltpu.make_async_copy(req_land, served, local_sem.at[0])
    to_scalar.start()
    to_scalar.wait()

    def make_page(d):
        page_send[d] = pages[served[d, 0, 0]]
        send_page(d).start()

    each(1, n, make_page)
    page_land[0] = pages[served[0, 0, 0]]

    inner[0] = tdot(tiles[0, 1], pages[0]) + tdot(tiles[1, 0], pages[1])
    inner[nb - 1] = tdot(tiles[nb - 1, 1], pages[nb - 1]) + tdot(tiles[nb - 2, 2], pages[nb - 2])

    def adjoint(m):
        column = jnp.concatenate([tiles[m - 1, 2], tiles[m, 1], tiles[m + 1, 0]], axis=0)
        inner[m] = tdot(column, pages[pl.ds(m - 1, 3)].reshape(3 * tile, fh))

    by(2, nb - 2, lambda i: adjoint(i + 1))

    def relate(key, prev, last):
        def latest(value, bound):
            def look(j, best):
                return jnp.where((key[j] == value) & (j < bound), j + 1, best)

            best = jnp.int32(0)
            if n > 16:
                return lax.fori_loop(0, n, look, best)
            for j in range(n):
                best = look(j, best)
            return best

        def before(d):
            prev[d] = latest(key[d], d)

        def final(r):
            last[r] = latest(r, n)

        each(0, n, before)
        each(0, nb, final)

    def chained(arrive, term, prev):
        def several(i, first=0):
            spots = [i * batch + j for j in range(batch)]
            for d in spots[first:]:
                arrive(d).wait_recv()
            terms = [term(d) for d in spots]
            for d, value in zip(spots, terms):
                links[d + 1] = value + links[prev[d]]

        several(0, 1)
        each(1, n // batch, several)

    def off_term(land):
        return lambda d: dot(offs[ahead(d)], land[d])

    chunk = label.shape[2]
    lane = lax.broadcasted_iota(jnp.int32, (chunk, chunk), 1)

    def build_hot(i):
        rows = pl.ds(pl.multiple_of(i * chunk, chunk), chunk)
        wanted = jnp.broadcast_to(label[i], (chunk, chunk)).T
        for c in range(nb * tile // chunk):
            hot[rows, c * chunk : (c + 1) * chunk] = jnp.where(
                wanted == lane + c * chunk, 1.0, 0.0
            ).astype(bf16)

    def clear_ends(field):
        @pl.when(b == 0)
        def _():
            field[0] = jnp.zeros((tile, fh), bf16)

        @pl.when(b == n - 1)
        def _():
            field[nb + 1] = jnp.zeros((tile, fh), bf16)

    def near(field):
        def line(r):
            weights = jnp.concatenate([tiles[r, 0], tiles[r, 1], tiles[r, 2]], axis=1)
            acc[r] = dot(weights, field[pl.ds(r, 3)].reshape(3 * tile, fh))

        by(4, nb, line)

    def set_keys(d):
        off_key[d] = off_row[ahead(d)]
        ask_key[d] = served[d, 0, 0]

    each(0, n, set_keys)
    relate(ask_key, ask_prev, ask_last)
    relate(off_key, off_prev, off_last)
    links[0] = jnp.zeros((tile, fh), f32)
    for copy in rims:
        copy.wait()
    inner[nb - 1] += jnp.where(b < n - 1, 1.0, 0.0) * rim_land[0]
    inner[0] += jnp.where(b > 0, 1.0, 0.0) * rim_land[1]
    each(0, hot.shape[0] // chunk, build_hot)

    def copy_pages(r):
        pad[r + 1] = pages[r]

    by(4, nb, copy_pages)
    for copy in page_edges:
        copy.wait()
    clear_ends(pad)
    near(pad)

    chained(send_back, lambda d: back_land[d].astype(f32), ask_prev)
    each(1, n, lambda d: send_back(d).wait_send())

    def round_t(r):
        block = (inner[r] + links[ask_last[r]]).astype(bf16)
        padt[r + 1] = block
        prop_t[r] = block

    by(4, nb, round_t)
    t_edges = edges((padt.at[1], padt.at[nb]), padt, 4)
    for copy in t_edges:
        copy.start()

    def make_t(d):
        back_send[d] = prop_t[served[d, 0, 0]]
        send_t(d).start()

    each(1, n, make_t)
    t_land[0] = prop_t[served[0, 0, 0]]
    stores[1].start()

    def lines(core):
        return pl.ds(pl.multiple_of(core * half, half), half)

    def columns(j, core):
        return pl.ds(pl.multiple_of((2 * j + core) * fh, fh), fh)

    def give(j):
        return remote(sel.at[j], feats.at[:, columns(j, h)], s_pick.at[j], r_pick.at[j], dp=o)

    def taken(j):
        spot = feats.at[:, columns(j, o)]
        return remote(sel.at[j], spot, s_pick.at[j], r_pick.at[j], dp=o)

    def flat(field):
        return field[...].reshape(nb * tile, fh)

    chained(send_page, off_term(page_land), off_prev)

    def round_a(r):
        prop_a[r] = (acc[r] + links[off_last[r]]).astype(bf16)

    by(4, nb, round_a)
    stores[0].start()
    both = jnp.concatenate([flat(prop_a), flat(prop_t)], axis=1)
    theirs = dot(hot[lines(o)], both).astype(bf16)
    for j in range(2):
        sel[j] = theirs[:, j * fh : (j + 1) * fh]
        give(j).start()
    ours = dot(hot[lines(h)], both).astype(bf16)
    for j in range(2):
        feats[:, columns(j, h)] = ours[:, j * fh : (j + 1) * fh]
    for copy in t_edges:
        copy.wait()
    clear_ends(padt)
    near(padt)
    loads[3].wait()
    loads[4].wait()
    for j in range(2):
        taken(j).wait_recv()
    early()
    chained(send_t, off_term(t_land), off_prev)

    def round_aat(r):
        prop_aat[r] = (acc[r] + links[off_last[r]]).astype(bf16)

    by(4, nb, round_aat)
    stores[2].start()
    whole = flat(prop_aat)
    sel[2] = dot(hot[lines(o)], whole).astype(bf16)
    give(2).start()
    feats[:, columns(2, h)] = dot(hot[lines(h)], whole).astype(bf16)
    taken(2).wait_recv()

    def finish(d):
        ask(d).wait_send()
        send_page(d).wait_send()
        send_t(d).wait_send()
        return 0

    def close():
        each(1, n, finish)
        for j in range(3):
            give(j).wait_send()
            stores[j].wait()

    return close


def whole_kernel(
    n, g, depth, split, by_rows, counts, pages_at, tiles_at, offs_at, w1_at, w2_at,
    off_row, req, label_page, labels, out_a, out_t, out_aat, grad1, grad2,
    w1, w2, feats, sel, *rest,
):
    train, spread = rest[: counts[0]], rest[counts[0] :]
    early, late = training(
        g, depth, split, by_rows, feats, sel, w1, w2, labels, grad1, grad2, *train
    )
    close = propagate(
        n, pages_at, tiles_at, offs_at, w1_at, w2_at, off_row, req, label_page,
        out_a, out_t, out_aat, *spread[:6], w1, w2, feats, sel, *spread[6:], early,
    )
    late()
    close()


def trained(pages, band_tiles, off_tiles, off_row, requests, label_page, labels, w_first, w_second):
    n = lax.axis_size("band")
    g = max(1, round((n / 2) ** (1 / 3)))
    if n % (g * g):
        g = 1
    depth = n // (g * g)
    hid, classes = w_second.shape
    tile = band_tiles.shape[-1]
    rows, fh = pages.shape
    nb = rows // tile
    count = labels.shape[0]
    in_f = w_first.shape[0]
    top, low = in_f // 2, hid // 2
    picks = top // fh
    half = (w_first.size + w_second.size) // (2 * hid)
    rows2 = half // (g * g)
    by_rows = rows2 % (16 * depth) == 0
    chunks = max(1, hid // 256 if by_rows else hid // (128 * depth))
    broad = hid // chunks
    split = SPLIT if by_rows else 1
    pieces, width = chunks * split, broad // split
    f32, bf16, i16 = jnp.float32, jnp.bfloat16, jnp.int16
    tall, thin = (rows2 // depth, width) if by_rows else (rows2, width // depth)
    vmem = pl.BlockSpec(memory_space=pltpu.VMEM)
    smem = pl.BlockSpec(memory_space=pltpu.SMEM)
    anywhere = pl.BlockSpec(memory_space=pl.ANY)
    dma = pltpu.SemaphoreType.DMA
    side, deep = max(1, g - 1), max(1, depth - 1)
    near, far = dma((pieces, side)), dma((pieces, deep))
    first = pltpu.VMEM((pieces, side, half // g + 16, width), i16)
    second = pltpu.VMEM((pieces, side, rows2 + 16, width), i16)
    third = pltpu.VMEM((pieces, deep, tall, thin), i16)
    powers = pltpu.VMEM((pieces, deep, 1, thin), f32)
    blocks = jax.ShapeDtypeStruct((nb, tile, fh), bf16)
    slots, blocked = pltpu.SMEM((n,), jnp.int32), pltpu.SMEM((nb,), jnp.int32)
    per_band = pltpu.VMEM((n, tile, fh), bf16)
    padded = pltpu.VMEM((nb + 2, tile, fh), bf16)
    train = [
        pltpu.VMEM((2, chunks, half, broad), bf16),
        pltpu.VMEM((top, 2 * count), bf16),
        pltpu.VMEM((count, hid), bf16),
        pltpu.VMEM((count, low), bf16),
        pltpu.VMEM((2, count, classes), bf16),
        pltpu.VMEM((chunks, 2, count, broad), bf16),
        pltpu.VMEM((count, hid), f32),
        pltpu.VMEM((chunks, half, broad), f32),
        first, first, second, second, third, third, powers, powers,
        dma((2,)), dma((2,)), dma((chunks,)), dma((chunks,)),
        near, near, near, near, far, far, far, far, far, far, near, near, near, near,
        dma((pieces,)), dma((pieces,)),
        dma((2, chunks, picks + max(1, broad // classes))),
    ]
    held = pltpu.VMEM((nb, tile, fh), bf16)
    prop_a, prop_t, prop_aat, grad1, grad2 = pl.pallas_call(
        functools.partial(whole_kernel, n, g, depth, split, by_rows, (len(train),)),
        out_shape=(
            blocks, blocks, blocks,
            jax.ShapeDtypeStruct(w_first.shape, bf16),
            jax.ShapeDtypeStruct(w_second.shape, bf16),
        ),
        in_specs=[anywhere] * 5 + [smem, smem, vmem, vmem],
        out_specs=(anywhere,) * 5,
        scratch_shapes=[
            pltpu.VMEM(w_first.shape, bf16),
            pltpu.VMEM(w_second.shape, bf16),
            pltpu.VMEM((count, in_f), bf16),
            pltpu.VMEM((picks, count, fh), bf16),
            *train,
            held, held, held, held,
            pltpu.VMEM(band_tiles.shape, bf16),
            pltpu.VMEM(off_tiles.shape, bf16),
            pltpu.VMEM((2 * count, rows), bf16),
            pltpu.VMEM((n + 1, tile, fh), f32),
            per_band, per_band, per_band, per_band, per_band,
            padded, padded,
            pltpu.VMEM((2, tile, fh), f32),
            pltpu.VMEM((2, tile, fh), f32),
            pltpu.VMEM((nb, tile, fh), f32),
            pltpu.VMEM((nb, tile, fh), f32),
            pltpu.VMEM((n, 1, 128), jnp.int32),
            pltpu.VMEM((n, 1, 128), jnp.int32),
            pltpu.SMEM((n, 1, 128), jnp.int32),
            slots, slots, blocked, slots, slots, blocked,
            dma((8,)), dma((1,)),
            *([dma((n,))] * 8), dma((6,)), dma((6,)), dma((picks,)), dma((picks,)),
        ],
        compiler_params=pltpu.CompilerParams(
            collective_id=0, has_side_effects=True, vmem_limit_bytes=(58 if n <= 16 else 62) * 2**20
        ),
        name="train",
    )(
        pages.reshape(nb, tile, fh),
        band_tiles,
        off_tiles,
        w_first,
        w_second,
        off_row,
        requests,
        label_page.reshape(2 * count // 128, 1, 128),
        labels.reshape(count // 128, 1, 128),
    )
    return (
        prop_a.reshape(rows, fh), prop_t.reshape(rows, fh), prop_aat.reshape(rows, fh), grad1, grad2
    )


def hand_out(*refs):
    sources, targets, held, come, leave = refs[:5], refs[5:10], refs[10:15], refs[15], refs[16]
    steps = []
    for i, (source, target, middle) in enumerate(zip(sources, targets, held)):
        size = source.shape[0] // 2
        for j in range(2):
            rows = pl.ds(j * size, size)
            steps.append(
                (
                    pltpu.make_async_copy(source.at[rows], middle.at[rows], come.at[i, j]),
                    pltpu.make_async_copy(middle.at[rows], target.at[rows], leave.at[i, j]),
                )
            )
    for first, _ in steps:
        first.start()
    for first, second in steps:
        first.wait()
        second.start()
    for _, second in steps:
        second.wait()


def handed_out(*arrays):
    anywhere = pl.BlockSpec(memory_space=pl.ANY)
    dma = pltpu.SemaphoreType.DMA
    return pl.pallas_call(
        hand_out,
        out_shape=tuple(jax.ShapeDtypeStruct(a.shape, a.dtype) for a in arrays),
        in_specs=[anywhere] * 5,
        out_specs=(anywhere,) * 5,
        scratch_shapes=[
            *(pltpu.VMEM(a.shape, a.dtype) for a in arrays), dma((5, 2)), dma((5, 2))
        ],
        name="hand_out",
    )(*arrays)


def per_device(
    pages, band_tiles, off_tiles, off_row, requests, label_page, labels, w_first, w_second
):
    results = trained(
        pages, band_tiles, off_tiles, off_row, requests, label_page, labels, w_first, w_second
    )
    return handed_out(*results)


def solution(mesh):
    placed = (
        P("band", "dp"),
        P("band", None, None, None),
        P("band", None, None),
        P("band"),
        P("band"),
        P("band"),
        P(("band", "dp")),
        P(),
        P(),
    )
    return jax.shard_map(
        per_device,
        mesh=mesh,
        in_specs=placed,
        out_specs=(P("band", "dp"), P("band", "dp"), P("band", "dp"), P(), P()),
        check_vma=False,
    )
```

```python
import functools

import jax
import jax.numpy as jnp
from jax import lax
from jax.experimental import pallas as pl
from jax.experimental.pallas import tpu as pltpu
from jax.sharding import PartitionSpec as P


MESH = pl.DeviceIdType.MESH
PACE = 3.2
SPLIT = 2


def greet(n):
    b, other = lax.axis_index("band"), 1 - lax.axis_index("dp")
    barrier = pltpu.get_barrier_semaphore()
    pl.semaphore_signal(barrier, inc=1, device_id={"dp": other}, device_id_type=MESH)

    def call(d, _):
        pl.semaphore_signal(
            barrier, inc=1, device_id={"band": lax.rem(b + d, n)}, device_id_type=MESH
        )
        return 0

    lax.fori_loop(1, n, call, 0)


def met(n):
    pl.semaphore_wait(pltpu.get_barrier_semaphore(), n)


def remote(src, dst, send_sem, recv_sem, **where):
    return pltpu.make_async_remote_copy(
        src_ref=src, dst_ref=dst, send_sem=send_sem, recv_sem=recv_sem,
        device_id=where, device_id_type=MESH,
    )


def each(start, stop, body):
    def step(d, _):
        body(d)
        return 0

    lax.fori_loop(start, stop, step, 0)


def by(step, stop, body):
    if stop % step:
        return each(0, stop, body)

    def several(i):
        for j in range(step):
            body(i * step + j)

    each(0, stop // step, several)


def training(
    g, depth, split, by_rows, feats, mine, w1, w2, label, grad1, grad2, out,
    feat_t, hid, hid_in, err, back, slope, cur, q1s, q1r, q2s, q2r, q3s, q3r, p3s, p3r,
    s_act, r_act, s_back, r_back, s_one, r_one, s_two, r_two, s_z, r_z, s_pz, r_pz,
    s_gz, r_gz, s_g2, r_g2, s_g1, r_g1, s_fw, r_fw, s_out,
):
    n = g * g * depth
    b, h = lax.axis_index("band"), lax.axis_index("dp")
    o = 1 - h
    x, y, z = lax.rem(b, g), lax.rem(lax.div(b, g), g), lax.div(b, g * g)
    c1, c2 = x + h * (y - x), y + h * (x - y)
    stride1, stride2 = 1 + h * (g - 1), g - h * (g - 1)
    count, classes = feats.shape[0], w2.shape[1]
    picks, _, fh = mine.shape
    chunks, half, broad = cur.shape
    pieces, width = chunks * split, broad // split
    low = hid_in.shape[1]
    top = picks * fh
    quarter = half - top
    low_step = low // chunks
    rows1 = half // g
    rows2 = rows1 // g
    base1 = c1 * rows1
    base2 = base1 + c2 * rows2
    tall, thin = (rows2 // depth, width) if by_rows else (rows2, width // depth)
    f32, bf16, i16 = jnp.float32, jnp.bfloat16, jnp.int16
    fine = 14.0

    def down(start, size):
        return pl.ds(pl.multiple_of(start, 16), size)

    def across(start, size):
        return pl.ds(pl.multiple_of(start, 128), size)

    def member1(d):
        m = lax.rem(c1 + d, g)
        return m, b + (m - c1) * stride1

    def member2(d):
        m = lax.rem(c2 + d, g)
        return m, b + (m - c2) * stride2

    def member_z(d):
        m = lax.rem(z + d, depth)
        return m, b + (m - z) * (g * g)

    def wide(p):
        return pl.ds(p % split * width, width)

    def spot_z(p, m):
        if by_rows:
            return down(base2 + m * tall, tall), wide(p)
        return down(base2, rows2), across(p % split * width + m * thin, thin)

    def encode(value, ref, scale=None):
        rows, cols = value.shape
        most = jnp.max(jnp.abs(value), axis=0, keepdims=True)
        power = jnp.floor(jnp.log2(jnp.maximum(most, 1e-33))) + 1.0
        whole = jnp.round(value * jnp.exp2(fine - power)).astype(jnp.int32)
        ref[:rows] = whole.astype(i16)
        if scale is None:
            ref[rows:] = jnp.broadcast_to(power, (16, cols)).astype(jnp.int32).astype(i16)
        else:
            scale[...] = power

    def decode(ref, scale=None):
        if scale is not None:
            return ref[...].astype(jnp.int32).astype(f32) * jnp.exp2(scale[...] - fine)
        rows = ref.shape[0] - 16
        power = ref[rows:].astype(jnp.int32).astype(f32)[:1]
        return ref[:rows].astype(jnp.int32).astype(f32) * jnp.exp2(power - fine)

    def hidden_copy():
        return remote(hid.at[:, across(o * low, low)], hid_in, s_act.at[0], r_act.at[0], dp=o)

    def error_copy():
        return remote(err.at[0], err.at[1], s_act.at[1], r_act.at[1], dp=o)

    def back_copy(p):
        return remote(back.at[p, 0], back.at[p, 1], s_back.at[p], r_back.at[p], dp=o)

    def one(p, d):
        return remote(
            q1s.at[p, d - 1], q1r.at[p, d - 1], s_one.at[p, d - 1], r_one.at[p, d - 1],
            band=member1(d)[1],
        )

    def two(p, d):
        return remote(
            q2s.at[p, d - 1], q2r.at[p, d - 1], s_two.at[p, d - 1], r_two.at[p, d - 1],
            band=member2(d)[1],
        )

    def along_z(p, d):
        return remote(
            q3s.at[p, d - 1], q3r.at[p, d - 1], s_z.at[p, d - 1], r_z.at[p, d - 1],
            band=member_z(d)[1],
        )

    def power_z(p, d):
        return remote(
            p3s.at[p, d - 1], p3r.at[p, d - 1], s_pz.at[p, d - 1], r_pz.at[p, d - 1],
            band=member_z(d)[1],
        )

    def back_z(p, d, taking=False):
        m, t = member_z(d)
        owner = lax.rem(z + depth - d, depth) if taking else z
        rows, cols = spot_z(p, owner)
        spot = out.at[h, p // split, rows, cols]
        return remote(spot, spot, s_gz.at[p, d - 1], r_gz.at[p, d - 1], band=t)

    def back2(p, d, taking=False):
        m, t = member2(d)
        owner = lax.rem(c2 + g - d, g) if taking else c2
        spot = out.at[h, p // split, down(base1 + owner * rows2, rows2), wide(p)]
        return remote(spot, spot, s_g2.at[p, d - 1], r_g2.at[p, d - 1], band=t)

    def back1(p, d, taking=False):
        m, t = member1(d)
        owner = lax.rem(c1 + g - d, g) if taking else c1
        spot = out.at[h, p // split, down(owner * rows1, rows1), wide(p)]
        return remote(spot, spot, s_g1.at[p, d - 1], r_g1.at[p, d - 1], band=t)

    def forward(p, core):
        spot = out.at[core, p // split, :, wide(p)]
        return remote(spot, spot, s_fw.at[p], r_fw.at[p], dp=o)

    def dot(lhs, rhs, i, j):
        return lax.dot_general(lhs, rhs, (((i,), (j,)), ((), ())), preferred_element_type=f32)

    def writes(core, q):
        target = pl.ds(q * broad, broad)
        copies = [
            pltpu.make_async_copy(
                out.at[core, q, pl.ds(j * fh, fh)],
                grad1.at[across((2 * j + core) * fh, fh), target],
                s_out.at[core, q, j],
            )
            for j in range(picks)
        ]
        for j in range(low_step // quarter):
            start = core * low + q * low_step + j * quarter
            copies.append(
                pltpu.make_async_copy(
                    out.at[core, q, pl.ds(top, quarter), pl.ds(j * classes, classes)],
                    grad2.at[down(start, quarter)],
                    s_out.at[core, q, picks + j],
                )
            )
        return copies

    def errors_back(q):
        w = slice(q * broad, (q + 1) * broad)
        signal = dot(err[0], w2[w], 1, 1) * slope[:, w]
        back[q, 0] = signal.astype(bf16)
        back_copy(q).start()

    def gradients(q):
        back_copy(q).wait_recv()
        cur[q, :top] = dot(feat_t[...], back[q].reshape(2 * count, broad), 1, 0)
        if q == 0:
            for copy in (hidden_copy(), error_copy()):
                copy.wait_recv()
        for j in range(low_step // quarter):
            start = q * low_step + j * quarter
            cur[q, top:, j * classes : (j + 1) * classes] = dot(
                hid[:, across(h * low + start, quarter)], err[0], 0, 0
            ) + dot(hid_in[:, start : start + quarter], err[1], 0, 0)
        for p in range(q * split, (q + 1) * split):
            for d in range(1, g):
                rows = down(member1(d)[0] * rows1, rows1)
                encode(cur[q, rows, wide(p)], q1s.at[p, d - 1])
                one(p, d).start()

    def after_one(p):
        q = p // split
        for d in range(1, g):
            one(p, d).wait_recv()
            cur[q, down(base1, rows1), wide(p)] += decode(q1r.at[p, d - 1])
        for d in range(1, g):
            rows = down(base1 + member2(d)[0] * rows2, rows2)
            encode(cur[q, rows, wide(p)], q2s.at[p, d - 1])
            two(p, d).start()

    def after_two(p):
        q = p // split
        for d in range(1, g):
            two(p, d).wait_recv()
            cur[q, down(base2, rows2), wide(p)] += decode(q2r.at[p, d - 1])
        for d in range(1, depth):
            rows, cols = spot_z(p, member_z(d)[0])
            encode(cur[q, rows, cols], q3s.at[p, d - 1], p3s.at[p, d - 1])
            along_z(p, d).start()
            power_z(p, d).start()

    def after_z(p):
        rows, cols = spot_z(p, z)
        total = cur[p // split, rows, cols]
        for d in range(1, depth):
            along_z(p, d).wait_recv()
            power_z(p, d).wait_recv()
            total += decode(q3r.at[p, d - 1], p3r.at[p, d - 1])
        out[h, p // split, rows, cols] = total.astype(bf16)
        for d in range(1, depth):
            back_z(p, d).start()

    def after_back_z(p):
        for d in range(1, depth):
            back_z(p, d, True).wait_recv()
        for d in range(1, g):
            back2(p, d).start()

    def after_back2(p):
        for d in range(1, g):
            back2(p, d, True).wait_recv()
        for d in range(1, g):
            back1(p, d).start()

    def after_back1(p):
        for d in range(1, g):
            back1(p, d, True).wait_recv()
        forward(p, h).start()
        if (p + 1) % split == 0:
            for copy in writes(h, p // split):
                copy.start()

    def after_forward(p):
        forward(p, o).wait_recv()
        if (p + 1) % split == 0:
            for copy in writes(o, p // split):
                copy.start()

    span = label.shape[2]
    lane = lax.broadcasted_iota(jnp.int32, (span, span), 1)
    step = min(broad, 256)
    parts = [slice(c * step, (c + 1) * step) for c in range(hid.shape[1] // step)]
    known = 2 * (picks - 1) * fh

    def turn(j):
        feat_t[j * fh : (j + 1) * fh, :count] = feats[:, across((2 * j + h) * fh, fh)].T
        feat_t[j * fh : (j + 1) * fh, count:] = mine[j].T

    def early():
        for w in parts:
            slope[:, w] = dot(feats[:, :known], w1[:known, w], 1, 0)
        for j in range(picks - 1):
            turn(j)

    def forward_pass():
        for w in parts:
            pre = slope[:, w] + dot(feats[:, known:], w1[known:, w], 1, 0)
            sigma = jax.nn.sigmoid(pre)
            hid[:, w] = (pre * sigma).astype(bf16)
            slope[:, w] = sigma * (1.0 + pre * (1.0 - sigma))
        hidden_copy().start()
        for i in range(count // span):
            rows = slice(i * span, (i + 1) * span)
            logits = dot(hid[rows], w2[...], 1, 0)
            powers = jnp.exp(logits - jnp.max(logits, axis=-1, keepdims=True))
            shares = powers / jnp.sum(powers, axis=-1, keepdims=True)
            wanted = jnp.broadcast_to(label[i], (span, span)).T
            label_hot = jnp.concatenate(
                [jnp.where(wanted == lane + c * span, 1.0, 0.0) for c in range(classes // span)],
                axis=1,
            )
            err[0, rows] = ((shares - label_hot) / (2 * count)).astype(bf16)
        error_copy().start()

    def late():
        forward_pass()
        turn(picks - 1)
        stages = (
            after_one, after_two, after_z, after_back_z, after_back2, after_back1, after_forward
        )
        plan = []
        for q in range(chunks):
            plan.append((q * split * 1.0, errors_back, q))
            plan.append((q * split + PACE, gradients, q))
        for p in range(pieces):
            for i, stage in enumerate(stages):
                plan.append((p + (i + 2) * PACE, stage, p))
        plan.sort(key=lambda item: item[0])
        for _, stage, p in plan:
            stage(p)
        for copy in (hidden_copy(), error_copy()):
            copy.wait_send()
        for q in range(chunks):
            back_copy(q).wait_send()
            for core in range(2):
                for copy in writes(core, q):
                    copy.wait()
        for p in range(pieces):
            for d in range(1, g):
                for copy in (one(p, d), two(p, d), back2(p, d), back1(p, d)):
                    copy.wait_send()
            for d in range(1, depth):
                along_z(p, d).wait_send()
                power_z(p, d).wait_send()
                back_z(p, d).wait_send()
            forward(p, h).wait_send()

    return early, late


def propagate(
    n, pages_at, tiles_at, offs_at, w1_at, w2_at, off_row, req, label,
    out_a, out_t, out_aat, prop_a, prop_t, prop_aat, pages, tiles, offs, w1, w2, feats, sel, hot, links,
    back_send, back_land, page_send, page_land, t_land, pad, padt,
    rim_send, rim_land, inner, acc, req_out, req_land, served, off_key, off_prev, off_last, ask_key, ask_prev, ask_last, load_sem, local_sem,
    s_req, r_req, s_back, r_back, s_page, r_page, s_t, r_t, s_edge, r_edge, s_pick, r_pick,
    early,
):
    b, h = lax.axis_index("band"), lax.axis_index("dp")
    o = 1 - h
    nb, tile, fh = pages.shape
    left, right = lax.rem(b + n - 1, n), lax.rem(b + 1, n)
    half = feats.shape[0]
    f32, bf16 = jnp.float32, jnp.bfloat16
    batch = 4 if n % 4 == 0 else 1

    def ahead(d):
        return lax.rem(b + d, n)

    def behind(d):
        return lax.rem(b + n - d, n)

    def tdot(x, y):
        return lax.dot_general(x, y, (((0,), (0,)), ((), ())), preferred_element_type=f32)

    def dot(x, y):
        return jnp.dot(x, y, preferred_element_type=f32)

    loads = [
        pltpu.make_async_copy(source, target, load_sem.at[i])
        for i, (source, target) in enumerate(
            ((pages_at, pages), (offs_at, offs), (tiles_at, tiles), (w1_at, w1), (w2_at, w2))
        )
    ]
    stores = [
        pltpu.make_async_copy(source, target, load_sem.at[len(loads) + i])
        for i, (source, target) in enumerate(((prop_a, out_a), (prop_t, out_t), (prop_aat, out_aat)))
    ]
    greet(n)
    for load in loads:
        load.start()

    def ask(d):
        t = ahead(d)
        return remote(req_out.at[t], req_land.at[d], s_req.at[d], r_req.at[d], band=t)

    def send_back(d):
        return remote(back_send.at[d], back_land.at[d], s_back.at[d], r_back.at[d], band=ahead(d))

    def send_page(d):
        return remote(page_send.at[d], page_land.at[d], s_page.at[d], r_page.at[d], band=behind(d))

    def send_t(d):
        return remote(back_send.at[d], t_land.at[d], s_t.at[d], r_t.at[d], band=behind(d))

    def edges(source, field, i):
        first, last = source
        return (
            remote(first, field.at[nb + 1], s_edge.at[i], r_edge.at[i], band=left),
            remote(last, field.at[0], s_edge.at[i + 1], r_edge.at[i + 1], band=right),
        )

    def build_req(t):
        req_out[t] = jnp.full((1, 128), req[t], jnp.int32)

    each(0, n, build_req)
    loads[0].wait()
    loads[1].wait()

    def make_back(d):
        k = ahead(d)
        back_send[d] = tdot(offs[k], pages[off_row[k]]).astype(bf16)

    met(n)
    each(1, n, lambda d: ask(d).start())

    def make_some(i):
        for j in range(batch):
            make_back(i * batch + j)
        for j in range(batch):
            send_back(i * batch + j).start()

    for d in range(batch):
        make_back(d)
    for d in range(1, batch):
        send_back(d).start()
    each(1, n // batch, make_some)
    back_land[0] = back_send[0]
    req_land[0] = req_out[b]
    page_edges = edges((pages.at[0], pages.at[nb - 1]), pad, 0)
    for copy in page_edges:
        copy.start()
    loads[2].wait()
    rim_send[0] = tdot(tiles[0, 0], pages[0])
    rim_send[1] = tdot(tiles[nb - 1, 2], pages[nb - 1])
    rims = (
        remote(rim_send.at[0], rim_land.at[0], s_edge.at[2], r_edge.at[2], band=left),
        remote(rim_send.at[1], rim_land.at[1], s_edge.at[3], r_edge.at[3], band=right),
    )
    for copy in rims:
        copy.start()
    each(1, n, lambda d: ask(d).wait_recv())
    to_scalar = pltpu.make_async_copy(req_land, served, local_sem.at[0])
    to_scalar.start()
    to_scalar.wait()

    def make_page(d):
        page_send[d] = pages[served[d, 0, 0]]
        send_page(d).start()

    each(1, n, make_page)
    page_land[0] = pages[served[0, 0, 0]]

    inner[0] = tdot(tiles[0, 1], pages[0]) + tdot(tiles[1, 0], pages[1])
    inner[nb - 1] = tdot(tiles[nb - 1, 1], pages[nb - 1]) + tdot(tiles[nb - 2, 2], pages[nb - 2])

    def adjoint(m):
        column = jnp.concatenate([tiles[m - 1, 2], tiles[m, 1], tiles[m + 1, 0]], axis=0)
        inner[m] = tdot(column, pages[pl.ds(m - 1, 3)].reshape(3 * tile, fh))

    by(2, nb - 2, lambda i: adjoint(i + 1))

    def relate(key, prev, last):
        def latest(value, bound):
            def look(j, best):
                return jnp.where((key[j] == value) & (j < bound), j + 1, best)

            best = jnp.int32(0)
            if n > 16:
                return lax.fori_loop(0, n, look, best)
            for j in range(n):
                best = look(j, best)
            return best

        def before(d):
            prev[d] = latest(key[d], d)

        def final(r):
            last[r] = latest(r, n)

        each(0, n, before)
        each(0, nb, final)

    def chained(arrive, term, prev):
        def several(i, first=0):
            spots = [i * batch + j for j in range(batch)]
            for d in spots[first:]:
                arrive(d).wait_recv()
            terms = [term(d) for d in spots]
            for d, value in zip(spots, terms):
                links[d + 1] = value + links[prev[d]]

        several(0, 1)
        each(1, n // batch, several)

    def off_term(land):
        return lambda d: dot(offs[ahead(d)], land[d])

    chunk = label.shape[2]
    lane = lax.broadcasted_iota(jnp.int32, (chunk, chunk), 1)

    def build_hot(i):
        rows = pl.ds(pl.multiple_of(i * chunk, chunk), chunk)
        wanted = jnp.broadcast_to(label[i], (chunk, chunk)).T
        for c in range(nb * tile // chunk):
            hot[rows, c * chunk : (c + 1) * chunk] = jnp.where(
                wanted == lane + c * chunk, 1.0, 0.0
            ).astype(bf16)

    def clear_ends(field):
        @pl.when(b == 0)
        def _():
            field[0] = jnp.zeros((tile, fh), bf16)

        @pl.when(b == n - 1)
        def _():
            field[nb + 1] = jnp.zeros((tile, fh), bf16)

    def near(field):
        def line(r):
            weights = jnp.concatenate([tiles[r, 0], tiles[r, 1], tiles[r, 2]], axis=1)
            acc[r] = dot(weights, field[pl.ds(r, 3)].reshape(3 * tile, fh))

        by(4, nb, line)

    def set_keys(d):
        off_key[d] = off_row[ahead(d)]
        ask_key[d] = served[d, 0, 0]

    each(0, n, set_keys)
    relate(ask_key, ask_prev, ask_last)
    relate(off_key, off_prev, off_last)
    links[0] = jnp.zeros((tile, fh), f32)
    for copy in rims:
        copy.wait()
    inner[nb - 1] += jnp.where(b < n - 1, 1.0, 0.0) * rim_land[0]
    inner[0] += jnp.where(b > 0, 1.0, 0.0) * rim_land[1]
    each(0, hot.shape[0] // chunk, build_hot)

    def copy_pages(r):
        pad[r + 1] = pages[r]

    by(4, nb, copy_pages)
    for copy in page_edges:
        copy.wait()
    clear_ends(pad)
    near(pad)

    chained(send_back, lambda d: back_land[d].astype(f32), ask_prev)
    each(1, n, lambda d: send_back(d).wait_send())

    def round_t(r):
        block = (inner[r] + links[ask_last[r]]).astype(bf16)
        padt[r + 1] = block
        prop_t[r] = block

    by(4, nb, round_t)
    t_edges = edges((padt.at[1], padt.at[nb]), padt, 4)
    for copy in t_edges:
        copy.start()

    def make_t(d):
        back_send[d] = prop_t[served[d, 0, 0]]
        send_t(d).start()

    each(1, n, make_t)
    t_land[0] = prop_t[served[0, 0, 0]]
    stores[1].start()

    def lines(core):
        return pl.ds(pl.multiple_of(core * half, half), half)

    def columns(j, core):
        return pl.ds(pl.multiple_of((2 * j + core) * fh, fh), fh)

    def give(j):
        return remote(sel.at[j], feats.at[:, columns(j, h)], s_pick.at[j], r_pick.at[j], dp=o)

    def taken(j):
        spot = feats.at[:, columns(j, o)]
        return remote(sel.at[j], spot, s_pick.at[j], r_pick.at[j], dp=o)

    def flat(field):
        return field[...].reshape(nb * tile, fh)

    chained(send_page, off_term(page_land), off_prev)

    def round_a(r):
        prop_a[r] = (acc[r] + links[off_last[r]]).astype(bf16)

    by(4, nb, round_a)
    stores[0].start()
    both = jnp.concatenate([flat(prop_a), flat(prop_t)], axis=1)
    theirs = dot(hot[lines(o)], both).astype(bf16)
    for j in range(2):
        sel[j] = theirs[:, j * fh : (j + 1) * fh]
        give(j).start()
    ours = dot(hot[lines(h)], both).astype(bf16)
    for j in range(2):
        feats[:, columns(j, h)] = ours[:, j * fh : (j + 1) * fh]
    for copy in t_edges:
        copy.wait()
    clear_ends(padt)
    near(padt)
    loads[3].wait()
    loads[4].wait()
    for j in range(2):
        taken(j).wait_recv()
    early()
    chained(send_t, off_term(t_land), off_prev)

    def round_aat(r):
        prop_aat[r] = (acc[r] + links[off_last[r]]).astype(bf16)

    by(4, nb, round_aat)
    stores[2].start()
    whole = flat(prop_aat)
    sel[2] = dot(hot[lines(o)], whole).astype(bf16)
    give(2).start()
    feats[:, columns(2, h)] = dot(hot[lines(h)], whole).astype(bf16)
    taken(2).wait_recv()

    def finish(d):
        ask(d).wait_send()
        send_page(d).wait_send()
        send_t(d).wait_send()
        return 0

    def close():
        each(1, n, finish)
        for j in range(3):
            give(j).wait_send()
            stores[j].wait()

    return close


def whole_kernel(
    n, g, depth, split, by_rows, counts, pages_at, tiles_at, offs_at, w1_at, w2_at,
    off_row, req, label_page, labels, out_a, out_t, out_aat, grad1, grad2,
    w1, w2, feats, sel, *rest,
):
    train, spread = rest[: counts[0]], rest[counts[0] :]
    early, late = training(
        g, depth, split, by_rows, feats, sel, w1, w2, labels, grad1, grad2, *train
    )
    close = propagate(
        n, pages_at, tiles_at, offs_at, w1_at, w2_at, off_row, req, label_page,
        out_a, out_t, out_aat, *spread[:6], w1, w2, feats, sel, *spread[6:], early,
    )
    late()
    close()


def trained(pages, band_tiles, off_tiles, off_row, requests, label_page, labels, w_first, w_second):
    n = lax.axis_size("band")
    g = max(1, round((n / 2) ** (1 / 3)))
    if n % (g * g):
        g = 1
    depth = n // (g * g)
    hid, classes = w_second.shape
    tile = band_tiles.shape[-1]
    rows, fh = pages.shape
    nb = rows // tile
    count = labels.shape[0]
    in_f = w_first.shape[0]
    top, low = in_f // 2, hid // 2
    picks = top // fh
    half = (w_first.size + w_second.size) // (2 * hid)
    rows2 = half // (g * g)
    by_rows = rows2 % (16 * depth) == 0
    chunks = max(1, hid // 256 if by_rows else hid // (128 * depth))
    broad = hid // chunks
    split = SPLIT if by_rows else 1
    pieces, width = chunks * split, broad // split
    f32, bf16, i16 = jnp.float32, jnp.bfloat16, jnp.int16
    tall, thin = (rows2 // depth, width) if by_rows else (rows2, width // depth)
    vmem = pl.BlockSpec(memory_space=pltpu.VMEM)
    smem = pl.BlockSpec(memory_space=pltpu.SMEM)
    anywhere = pl.BlockSpec(memory_space=pl.ANY)
    dma = pltpu.SemaphoreType.DMA
    side, deep = max(1, g - 1), max(1, depth - 1)
    near, far = dma((pieces, side)), dma((pieces, deep))
    first = pltpu.VMEM((pieces, side, half // g + 16, width), i16)
    second = pltpu.VMEM((pieces, side, rows2 + 16, width), i16)
    third = pltpu.VMEM((pieces, deep, tall, thin), i16)
    powers = pltpu.VMEM((pieces, deep, 1, thin), f32)
    blocks = jax.ShapeDtypeStruct((nb, tile, fh), bf16)
    slots, blocked = pltpu.SMEM((n,), jnp.int32), pltpu.SMEM((nb,), jnp.int32)
    per_band = pltpu.VMEM((n, tile, fh), bf16)
    padded = pltpu.VMEM((nb + 2, tile, fh), bf16)
    train = [
        pltpu.VMEM((2, chunks, half, broad), bf16),
        pltpu.VMEM((top, 2 * count), bf16),
        pltpu.VMEM((count, hid), bf16),
        pltpu.VMEM((count, low), bf16),
        pltpu.VMEM((2, count, classes), bf16),
        pltpu.VMEM((chunks, 2, count, broad), bf16),
        pltpu.VMEM((count, hid), f32),
        pltpu.VMEM((chunks, half, broad), f32),
        first, first, second, second, third, third, powers, powers,
        dma((2,)), dma((2,)), dma((chunks,)), dma((chunks,)),
        near, near, near, near, far, far, far, far, far, far, near, near, near, near,
        dma((pieces,)), dma((pieces,)),
        dma((2, chunks, picks + max(1, broad // classes))),
    ]
    held = pltpu.VMEM((nb, tile, fh), bf16)
    prop_a, prop_t, prop_aat, grad1, grad2 = pl.pallas_call(
        functools.partial(whole_kernel, n, g, depth, split, by_rows, (len(train),)),
        out_shape=(
            blocks, blocks, blocks,
            jax.ShapeDtypeStruct(w_first.shape, bf16),
            jax.ShapeDtypeStruct(w_second.shape, bf16),
        ),
        in_specs=[anywhere] * 5 + [smem, smem, vmem, vmem],
        out_specs=(anywhere,) * 5,
        scratch_shapes=[
            pltpu.VMEM(w_first.shape, bf16),
            pltpu.VMEM(w_second.shape, bf16),
            pltpu.VMEM((count, in_f), bf16),
            pltpu.VMEM((picks, count, fh), bf16),
            *train,
            held, held, held, held,
            pltpu.VMEM(band_tiles.shape, bf16),
            pltpu.VMEM(off_tiles.shape, bf16),
            pltpu.VMEM((2 * count, rows), bf16),
            pltpu.VMEM((n + 1, tile, fh), f32),
            per_band, per_band, per_band, per_band, per_band,
            padded, padded,
            pltpu.VMEM((2, tile, fh), f32),
            pltpu.VMEM((2, tile, fh), f32),
            pltpu.VMEM((nb, tile, fh), f32),
            pltpu.VMEM((nb, tile, fh), f32),
            pltpu.VMEM((n, 1, 128), jnp.int32),
            pltpu.VMEM((n, 1, 128), jnp.int32),
            pltpu.SMEM((n, 1, 128), jnp.int32),
            slots, slots, blocked, slots, slots, blocked,
            dma((8,)), dma((1,)),
            *([dma((n,))] * 8), dma((6,)), dma((6,)), dma((picks,)), dma((picks,)),
        ],
        compiler_params=pltpu.CompilerParams(
            collective_id=0, has_side_effects=True, vmem_limit_bytes=(58 if n <= 16 else 62) * 2**20
        ),
        name="train",
    )(
        pages.reshape(nb, tile, fh),
        band_tiles,
        off_tiles,
        w_first,
        w_second,
        off_row,
        requests,
        label_page.reshape(2 * count // 128, 1, 128),
        labels.reshape(count // 128, 1, 128),
    )
    return (
        prop_a.reshape(rows, fh), prop_t.reshape(rows, fh), prop_aat.reshape(rows, fh), grad1, grad2
    )


def hand_out(*refs):
    sources, targets, held, come, leave = refs[:5], refs[5:10], refs[10:15], refs[15], refs[16]
    steps = []
    for i, (source, target, middle) in enumerate(zip(sources, targets, held)):
        size = source.shape[0] // 2
        for j in range(2):
            rows = pl.ds(j * size, size)
            steps.append(
                (
                    pltpu.make_async_copy(source.at[rows], middle.at[rows], come.at[i, j]),
                    pltpu.make_async_copy(middle.at[rows], target.at[rows], leave.at[i, j]),
                )
            )
    for first, _ in steps:
        first.start()
    for first, second in steps:
        first.wait()
        second.start()
    for _, second in steps:
        second.wait()


def handed_out(*arrays):
    anywhere = pl.BlockSpec(memory_space=pl.ANY)
    dma = pltpu.SemaphoreType.DMA
    return pl.pallas_call(
        hand_out,
        out_shape=tuple(jax.ShapeDtypeStruct(a.shape, a.dtype) for a in arrays),
        in_specs=[anywhere] * 5,
        out_specs=(anywhere,) * 5,
        scratch_shapes=[
            *(pltpu.VMEM(a.shape, a.dtype) for a in arrays), dma((5, 2)), dma((5, 2))
        ],
        name="hand_out",
    )(*arrays)


def per_device(
    pages, band_tiles, off_tiles, off_row, requests, label_page, labels, w_first, w_second
):
    results = trained(
        pages, band_tiles, off_tiles, off_row, requests, label_page, labels, w_first, w_second
    )
    return handed_out(*results)


def solution(mesh):
    placed = (
        P("band", "dp"),
        P("band", None, None, None),
        P("band", None, None),
        P("band"),
        P("band"),
        P("band"),
        P(("band", "dp")),
        P(),
        P(),
    )
    return jax.shard_map(
        per_device,
        mesh=mesh,
        in_specs=placed,
        out_specs=(P("band", "dp"), P("band", "dp"), P("band", "dp"), P(), P()),
        check_vma=False,
    )
```

```python
import functools

import jax
import jax.numpy as jnp
from jax import lax
from jax.experimental import pallas as pl
from jax.experimental.pallas import tpu as pltpu
from jax.sharding import PartitionSpec as P


MESH = pl.DeviceIdType.MESH
PACE = 3.2
SPLIT = 2


def greet(n):
    b, other = lax.axis_index("band"), 1 - lax.axis_index("dp")
    barrier = pltpu.get_barrier_semaphore()
    pl.semaphore_signal(barrier, inc=1, device_id={"dp": other}, device_id_type=MESH)

    def call(d, _):
        pl.semaphore_signal(
            barrier, inc=1, device_id={"band": lax.rem(b + d, n)}, device_id_type=MESH
        )
        return 0

    lax.fori_loop(1, n, call, 0)


def met(n):
    pl.semaphore_wait(pltpu.get_barrier_semaphore(), n)


def remote(src, dst, send_sem, recv_sem, **where):
    return pltpu.make_async_remote_copy(
        src_ref=src, dst_ref=dst, send_sem=send_sem, recv_sem=recv_sem,
        device_id=where, device_id_type=MESH,
    )


def each(start, stop, body):
    def step(d, _):
        body(d)
        return 0

    lax.fori_loop(start, stop, step, 0)


def by(step, stop, body):
    if stop % step:
        return each(0, stop, body)

    def several(i):
        for j in range(step):
            body(i * step + j)

    each(0, stop // step, several)


def training(
    g, depth, split, by_rows, feats, mine, w1, w2, label, grad1, grad2, out,
    feat_t, hid, hid_in, err, back, slope, cur, q1s, q1r, q2s, q2r, q3s, q3r, p3s, p3r,
    s_act, r_act, s_back, r_back, s_one, r_one, s_two, r_two, s_z, r_z, s_pz, r_pz,
    s_gz, r_gz, s_g2, r_g2, s_g1, r_g1, s_fw, r_fw, s_out,
):
    n = g * g * depth
    b, h = lax.axis_index("band"), lax.axis_index("dp")
    o = 1 - h
    x, y, z = lax.rem(b, g), lax.rem(lax.div(b, g), g), lax.div(b, g * g)
    c1, c2 = x + h * (y - x), y + h * (x - y)
    stride1, stride2 = 1 + h * (g - 1), g - h * (g - 1)
    count, classes = feats.shape[0], w2.shape[1]
    picks, _, fh = mine.shape
    chunks, half, broad = cur.shape
    pieces, width = chunks * split, broad // split
    low = hid_in.shape[1]
    top = picks * fh
    quarter = half - top
    low_step = low // chunks
    rows1 = half // g
    rows2 = rows1 // g
    base1 = c1 * rows1
    base2 = base1 + c2 * rows2
    tall, thin = (rows2 // depth, width) if by_rows else (rows2, width // depth)
    f32, bf16, i16 = jnp.float32, jnp.bfloat16, jnp.int16
    fine = 14.0

    def down(start, size):
        return pl.ds(pl.multiple_of(start, 16), size)

    def across(start, size):
        return pl.ds(pl.multiple_of(start, 128), size)

    def member1(d):
        m = lax.rem(c1 + d, g)
        return m, b + (m - c1) * stride1

    def member2(d):
        m = lax.rem(c2 + d, g)
        return m, b + (m - c2) * stride2

    def member_z(d):
        m = lax.rem(z + d, depth)
        return m, b + (m - z) * (g * g)

    def wide(p):
        return pl.ds(p % split * width, width)

    def spot_z(p, m):
        if by_rows:
            return down(base2 + m * tall, tall), wide(p)
        return down(base2, rows2), across(p % split * width + m * thin, thin)

    def encode(value, ref, scale=None):
        rows, cols = value.shape
        most = jnp.max(jnp.abs(value), axis=0, keepdims=True)
        power = jnp.floor(jnp.log2(jnp.maximum(most, 1e-33))) + 1.0
        whole = jnp.round(value * jnp.exp2(fine - power)).astype(jnp.int32)
        ref[:rows] = whole.astype(i16)
        if scale is None:
            ref[rows:] = jnp.broadcast_to(power, (16, cols)).astype(jnp.int32).astype(i16)
        else:
            scale[...] = power

    def decode(ref, scale=None):
        if scale is not None:
            return ref[...].astype(jnp.int32).astype(f32) * jnp.exp2(scale[...] - fine)
        rows = ref.shape[0] - 16
        power = ref[rows:].astype(jnp.int32).astype(f32)[:1]
        return ref[:rows].astype(jnp.int32).astype(f32) * jnp.exp2(power - fine)

    def hidden_copy():
        return remote(hid.at[:, across(o * low, low)], hid_in, s_act.at[0], r_act.at[0], dp=o)

    def error_copy():
        return remote(err.at[0], err.at[1], s_act.at[1], r_act.at[1], dp=o)

    def back_copy(p):
        return remote(back.at[p, 0], back.at[p, 1], s_back.at[p], r_back.at[p], dp=o)

    def one(p, d):
        return remote(
            q1s.at[p, d - 1], q1r.at[p, d - 1], s_one.at[p, d - 1], r_one.at[p, d - 1],
            band=member1(d)[1],
        )

    def two(p, d):
        return remote(
            q2s.at[p, d - 1], q2r.at[p, d - 1], s_two.at[p, d - 1], r_two.at[p, d - 1],
            band=member2(d)[1],
        )

    def along_z(p, d):
        return remote(
            q3s.at[p, d - 1], q3r.at[p, d - 1], s_z.at[p, d - 1], r_z.at[p, d - 1],
            band=member_z(d)[1],
        )

    def power_z(p, d):
        return remote(
            p3s.at[p, d - 1], p3r.at[p, d - 1], s_pz.at[p, d - 1], r_pz.at[p, d - 1],
            band=member_z(d)[1],
        )

    def back_z(p, d, taking=False):
        m, t = member_z(d)
        owner = lax.rem(z + depth - d, depth) if taking else z
        rows, cols = spot_z(p, owner)
        spot = out.at[h, p // split, rows, cols]
        return remote(spot, spot, s_gz.at[p, d - 1], r_gz.at[p, d - 1], band=t)

    def back2(p, d, taking=False):
        m, t = member2(d)
        owner = lax.rem(c2 + g - d, g) if taking else c2
        spot = out.at[h, p // split, down(base1 + owner * rows2, rows2), wide(p)]
        return remote(spot, spot, s_g2.at[p, d - 1], r_g2.at[p, d - 1], band=t)

    def back1(p, d, taking=False):
        m, t = member1(d)
        owner = lax.rem(c1 + g - d, g) if taking else c1
        spot = out.at[h, p // split, down(owner * rows1, rows1), wide(p)]
        return remote(spot, spot, s_g1.at[p, d - 1], r_g1.at[p, d - 1], band=t)

    def forward(p, core):
        spot = out.at[core, p // split, :, wide(p)]
        return remote(spot, spot, s_fw.at[p], r_fw.at[p], dp=o)

    def dot(lhs, rhs, i, j):
        return lax.dot_general(lhs, rhs, (((i,), (j,)), ((), ())), preferred_element_type=f32)

    def writes(core, q):
        target = pl.ds(q * broad, broad)
        copies = [
            pltpu.make_async_copy(
                out.at[core, q, pl.ds(j * fh, fh)],
                grad1.at[across((2 * j + core) * fh, fh), target],
                s_out.at[core, q, j],
            )
            for j in range(picks)
        ]
        for j in range(low_step // quarter):
            start = core * low + q * low_step + j * quarter
            copies.append(
                pltpu.make_async_copy(
                    out.at[core, q, pl.ds(top, quarter), pl.ds(j * classes, classes)],
                    grad2.at[down(start, quarter)],
                    s_out.at[core, q, picks + j],
                )
            )
        return copies

    def errors_back(q):
        w = slice(q * broad, (q + 1) * broad)
        signal = dot(err[0], w2[w], 1, 1) * slope[:, w]
        back[q, 0] = signal.astype(bf16)
        back_copy(q).start()

    def gradients(q):
        back_copy(q).wait_recv()
        cur[q, :top] = dot(feat_t[...], back[q].reshape(2 * count, broad), 1, 0)
        if q == 0:
            for copy in (hidden_copy(), error_copy()):
                copy.wait_recv()
        for j in range(low_step // quarter):
            start = q * low_step + j * quarter
            cur[q, top:, j * classes : (j + 1) * classes] = dot(
                hid[:, across(h * low + start, quarter)], err[0], 0, 0
            ) + dot(hid_in[:, start : start + quarter], err[1], 0, 0)
        for p in range(q * split, (q + 1) * split):
            for d in range(1, g):
                rows = down(member1(d)[0] * rows1, rows1)
                encode(cur[q, rows, wide(p)], q1s.at[p, d - 1])
                one(p, d).start()

    def after_one(p):
        q = p // split
        for d in range(1, g):
            one(p, d).wait_recv()
            cur[q, down(base1, rows1), wide(p)] += decode(q1r.at[p, d - 1])
        for d in range(1, g):
            rows = down(base1 + member2(d)[0] * rows2, rows2)
            encode(cur[q, rows, wide(p)], q2s.at[p, d - 1])
            two(p, d).start()

    def after_two(p):
        q = p // split
        for d in range(1, g):
            two(p, d).wait_recv()
            cur[q, down(base2, rows2), wide(p)] += decode(q2r.at[p, d - 1])
        for d in range(1, depth):
            rows, cols = spot_z(p, member_z(d)[0])
            encode(cur[q, rows, cols], q3s.at[p, d - 1], p3s.at[p, d - 1])
            along_z(p, d).start()
            power_z(p, d).start()

    def after_z(p):
        rows, cols = spot_z(p, z)
        total = cur[p // split, rows, cols]
        for d in range(1, depth):
            along_z(p, d).wait_recv()
            power_z(p, d).wait_recv()
            total += decode(q3r.at[p, d - 1], p3r.at[p, d - 1])
        out[h, p // split, rows, cols] = total.astype(bf16)
        for d in range(1, depth):
            back_z(p, d).start()
        for d in range(1, g):
            one(p, d).wait_send()
            two(p, d).wait_send()
        if p % split == 0:
            back_copy(p // split).wait_send()
        if p == 0:
            hidden_copy().wait_send()
            error_copy().wait_send()

    def after_back_z(p):
        for d in range(1, depth):
            back_z(p, d, True).wait_recv()
        for d in range(1, g):
            back2(p, d).start()
        for d in range(1, depth):
            along_z(p, d).wait_send()
            power_z(p, d).wait_send()

    def after_back2(p):
        for d in range(1, g):
            back2(p, d, True).wait_recv()
        for d in range(1, g):
            back1(p, d).start()

    def after_back1(p):
        for d in range(1, g):
            back1(p, d, True).wait_recv()
        forward(p, h).start()
        for d in range(1, depth):
            back_z(p, d).wait_send()
        for d in range(1, g):
            back2(p, d).wait_send()
        if (p + 1) % split == 0:
            for copy in writes(h, p // split):
                copy.start()

    def after_forward(p):
        forward(p, o).wait_recv()
        if (p + 1) % split == 0:
            for copy in writes(o, p // split):
                copy.start()
            if p >= split:
                for core in range(2):
                    for copy in writes(core, p // split - 1):
                        copy.wait()

    span = label.shape[2]
    lane = lax.broadcasted_iota(jnp.int32, (span, span), 1)
    step = min(broad, 256)
    parts = [slice(c * step, (c + 1) * step) for c in range(hid.shape[1] // step)]
    known = 2 * (picks - 1) * fh

    def turn(j):
        feat_t[j * fh : (j + 1) * fh, :count] = feats[:, across((2 * j + h) * fh, fh)].T
        feat_t[j * fh : (j + 1) * fh, count:] = mine[j].T

    def early():
        for w in parts:
            slope[:, w] = dot(feats[:, :known], w1[:known, w], 1, 0)
        for j in range(picks - 1):
            turn(j)

    def forward_pass():
        for w in parts:
            pre = slope[:, w] + dot(feats[:, known:], w1[known:, w], 1, 0)
            sigma = jax.nn.sigmoid(pre)
            hid[:, w] = (pre * sigma).astype(bf16)
            slope[:, w] = sigma * (1.0 + pre * (1.0 - sigma))
        hidden_copy().start()
        for i in range(count // span):
            rows = slice(i * span, (i + 1) * span)
            logits = dot(hid[rows], w2[...], 1, 0)
            powers = jnp.exp(logits - jnp.max(logits, axis=-1, keepdims=True))
            shares = powers / jnp.sum(powers, axis=-1, keepdims=True)
            wanted = jnp.broadcast_to(label[i], (span, span)).T
            label_hot = jnp.concatenate(
                [jnp.where(wanted == lane + c * span, 1.0, 0.0) for c in range(classes // span)],
                axis=1,
            )
            err[0, rows] = ((shares - label_hot) / (2 * count)).astype(bf16)
        error_copy().start()

    def late(close):
        forward_pass()
        turn(picks - 1)
        stages = (
            after_one, after_two, after_z, after_back_z, after_back2, after_back1, after_forward
        )
        plan = []
        for q in range(chunks):
            plan.append((q * split * 1.0, errors_back, q))
            plan.append((q * split + PACE, gradients, q))
        for p in range(pieces):
            for i, stage in enumerate(stages):
                plan.append((p + (i + 2) * PACE, stage, p))
        plan.sort(key=lambda item: item[0])
        closed = False
        for _, stage, p in plan:
            if stage is after_one and not closed:
                close()
                closed = True
            stage(p)
        for p in range(pieces):
            for d in range(1, g):
                back1(p, d).wait_send()
            forward(p, h).wait_send()
        for core in range(2):
            for copy in writes(core, chunks - 1):
                copy.wait()

    return early, late


def propagate(
    n, pages_at, tiles_at, offs_at, w1_at, w2_at, off_row, req, label,
    out_a, out_t, out_aat, prop_a, prop_t, prop_aat, pages, tiles, offs, w1, w2, feats, sel, hot, links,
    back_send, back_land, page_send, page_land, t_land, pad, padt,
    rim_send, rim_land, inner, acc, req_out, req_land, served, off_key, off_prev, off_last, ask_key, ask_prev, ask_last, load_sem, local_sem,
    s_req, r_req, s_back, r_back, s_page, r_page, s_t, r_t, s_edge, r_edge, s_pick, r_pick,
    early,
):
    b, h = lax.axis_index("band"), lax.axis_index("dp")
    o = 1 - h
    nb, tile, fh = pages.shape
    left, right = lax.rem(b + n - 1, n), lax.rem(b + 1, n)
    half = feats.shape[0]
    f32, bf16 = jnp.float32, jnp.bfloat16
    batch = 4 if n % 4 == 0 else 1

    def ahead(d):
        return lax.rem(b + d, n)

    def behind(d):
        return lax.rem(b + n - d, n)

    def tdot(x, y):
        return lax.dot_general(x, y, (((0,), (0,)), ((), ())), preferred_element_type=f32)

    def dot(x, y):
        return jnp.dot(x, y, preferred_element_type=f32)

    loads = [
        pltpu.make_async_copy(source, target, load_sem.at[i])
        for i, (source, target) in enumerate(
            ((pages_at, pages), (offs_at, offs), (tiles_at, tiles), (w1_at, w1), (w2_at, w2))
        )
    ]
    stores = [
        pltpu.make_async_copy(source, target, load_sem.at[len(loads) + i])
        for i, (source, target) in enumerate(((prop_a, out_a), (prop_t, out_t), (prop_aat, out_aat)))
    ]
    greet(n)
    for load in loads:
        load.start()

    def ask(d):
        t = ahead(d)
        return remote(req_out.at[t], req_land.at[d], s_req.at[d], r_req.at[d], band=t)

    def send_back(d):
        return remote(back_send.at[d], back_land.at[d], s_back.at[d], r_back.at[d], band=ahead(d))

    def send_page(d):
        return remote(page_send.at[d], page_land.at[d], s_page.at[d], r_page.at[d], band=behind(d))

    def send_t(d):
        return remote(back_send.at[d], t_land.at[d], s_t.at[d], r_t.at[d], band=behind(d))

    def edges(source, field, i):
        first, last = source
        return (
            remote(first, field.at[nb + 1], s_edge.at[i], r_edge.at[i], band=left),
            remote(last, field.at[0], s_edge.at[i + 1], r_edge.at[i + 1], band=right),
        )

    def build_req(t):
        req_out[t] = jnp.full((1, 128), req[t], jnp.int32)

    each(0, n, build_req)
    loads[0].wait()
    loads[1].wait()

    def make_back(d):
        k = ahead(d)
        back_send[d] = tdot(offs[k], pages[off_row[k]]).astype(bf16)

    met(n)
    each(1, n, lambda d: ask(d).start())

    def make_some(i):
        for j in range(batch):
            make_back(i * batch + j)
        for j in range(batch):
            send_back(i * batch + j).start()

    for d in range(batch):
        make_back(d)
    for d in range(1, batch):
        send_back(d).start()
    each(1, n // batch, make_some)
    back_land[0] = back_send[0]
    req_land[0] = req_out[b]
    page_edges = edges((pages.at[0], pages.at[nb - 1]), pad, 0)
    for copy in page_edges:
        copy.start()
    loads[2].wait()
    rim_send[0] = tdot(tiles[0, 0], pages[0])
    rim_send[1] = tdot(tiles[nb - 1, 2], pages[nb - 1])
    rims = (
        remote(rim_send.at[0], rim_land.at[0], s_edge.at[2], r_edge.at[2], band=left),
        remote(rim_send.at[1], rim_land.at[1], s_edge.at[3], r_edge.at[3], band=right),
    )
    for copy in rims:
        copy.start()
    each(1, n, lambda d: ask(d).wait_recv())
    to_scalar = pltpu.make_async_copy(req_land, served, local_sem.at[0])
    to_scalar.start()
    to_scalar.wait()

    def make_page(d):
        page_send[d] = pages[served[d, 0, 0]]
        send_page(d).start()

    each(1, n, make_page)
    page_land[0] = pages[served[0, 0, 0]]

    inner[0] = tdot(tiles[0, 1], pages[0]) + tdot(tiles[1, 0], pages[1])
    inner[nb - 1] = tdot(tiles[nb - 1, 1], pages[nb - 1]) + tdot(tiles[nb - 2, 2], pages[nb - 2])

    def adjoint(m):
        column = jnp.concatenate([tiles[m - 1, 2], tiles[m, 1], tiles[m + 1, 0]], axis=0)
        inner[m] = tdot(column, pages[pl.ds(m - 1, 3)].reshape(3 * tile, fh))

    by(2, nb - 2, lambda i: adjoint(i + 1))

    def relate(key, prev, last):
        def latest(value, bound):
            def look(j, best):
                return jnp.where((key[j] == value) & (j < bound), j + 1, best)

            best = jnp.int32(0)
            if n > 16:
                return lax.fori_loop(0, n, look, best)
            for j in range(n):
                best = look(j, best)
            return best

        def before(d):
            prev[d] = latest(key[d], d)

        def final(r):
            last[r] = latest(r, n)

        each(0, n, before)
        each(0, nb, final)

    def chained(arrive, term, prev):
        def several(i, first=0):
            spots = [i * batch + j for j in range(batch)]
            for d in spots[first:]:
                arrive(d).wait_recv()
            terms = [term(d) for d in spots]
            for d, value in zip(spots, terms):
                links[d + 1] = value + links[prev[d]]

        several(0, 1)
        each(1, n // batch, several)

    def off_term(land):
        return lambda d: dot(offs[ahead(d)], land[d])

    chunk = label.shape[2]
    lane = lax.broadcasted_iota(jnp.int32, (chunk, chunk), 1)

    def build_hot(i):
        rows = pl.ds(pl.multiple_of(i * chunk, chunk), chunk)
        wanted = jnp.broadcast_to(label[i], (chunk, chunk)).T
        for c in range(nb * tile // chunk):
            hot[rows, c * chunk : (c + 1) * chunk] = jnp.where(
                wanted == lane + c * chunk, 1.0, 0.0
            ).astype(bf16)

    def clear_ends(field):
        @pl.when(b == 0)
        def _():
            field[0] = jnp.zeros((tile, fh), bf16)

        @pl.when(b == n - 1)
        def _():
            field[nb + 1] = jnp.zeros((tile, fh), bf16)

    def near(field):
        def line(r):
            weights = jnp.concatenate([tiles[r, 0], tiles[r, 1], tiles[r, 2]], axis=1)
            acc[r] = dot(weights, field[pl.ds(r, 3)].reshape(3 * tile, fh))

        by(4, nb, line)

    def set_keys(d):
        off_key[d] = off_row[ahead(d)]
        ask_key[d] = served[d, 0, 0]

    each(0, n, set_keys)
    relate(ask_key, ask_prev, ask_last)
    relate(off_key, off_prev, off_last)
    links[0] = jnp.zeros((tile, fh), f32)
    for copy in rims:
        copy.wait()
    inner[nb - 1] += jnp.where(b < n - 1, 1.0, 0.0) * rim_land[0]
    inner[0] += jnp.where(b > 0, 1.0, 0.0) * rim_land[1]
    each(0, hot.shape[0] // chunk, build_hot)

    def copy_pages(r):
        pad[r + 1] = pages[r]

    by(4, nb, copy_pages)
    for copy in page_edges:
        copy.wait()
    clear_ends(pad)
    near(pad)

    chained(send_back, lambda d: back_land[d].astype(f32), ask_prev)
    each(1, n, lambda d: send_back(d).wait_send())

    def round_t(r):
        block = (inner[r] + links[ask_last[r]]).astype(bf16)
        padt[r + 1] = block
        prop_t[r] = block

    by(4, nb, round_t)
    t_edges = edges((padt.at[1], padt.at[nb]), padt, 4)
    for copy in t_edges:
        copy.start()

    def make_t(d):
        back_send[d] = prop_t[served[d, 0, 0]]
        send_t(d).start()

    each(1, n, make_t)
    t_land[0] = prop_t[served[0, 0, 0]]
    stores[1].start()

    def lines(core):
        return pl.ds(pl.multiple_of(core * half, half), half)

    def columns(j, core):
        return pl.ds(pl.multiple_of((2 * j + core) * fh, fh), fh)

    def give(j):
        return remote(sel.at[j], feats.at[:, columns(j, h)], s_pick.at[j], r_pick.at[j], dp=o)

    def taken(j):
        spot = feats.at[:, columns(j, o)]
        return remote(sel.at[j], spot, s_pick.at[j], r_pick.at[j], dp=o)

    def flat(field):
        return field[...].reshape(nb * tile, fh)

    chained(send_page, off_term(page_land), off_prev)

    def round_a(r):
        prop_a[r] = (acc[r] + links[off_last[r]]).astype(bf16)

    by(4, nb, round_a)
    stores[0].start()
    both = jnp.concatenate([flat(prop_a), flat(prop_t)], axis=1)
    theirs = dot(hot[lines(o)], both).astype(bf16)
    for j in range(2):
        sel[j] = theirs[:, j * fh : (j + 1) * fh]
        give(j).start()
    ours = dot(hot[lines(h)], both).astype(bf16)
    for j in range(2):
        feats[:, columns(j, h)] = ours[:, j * fh : (j + 1) * fh]
    for copy in t_edges:
        copy.wait()
    clear_ends(padt)
    near(padt)
    loads[3].wait()
    loads[4].wait()
    for j in range(2):
        taken(j).wait_recv()
    early()
    chained(send_t, off_term(t_land), off_prev)

    def round_aat(r):
        prop_aat[r] = (acc[r] + links[off_last[r]]).astype(bf16)

    by(4, nb, round_aat)
    stores[2].start()
    whole = flat(prop_aat)
    sel[2] = dot(hot[lines(o)], whole).astype(bf16)
    give(2).start()
    feats[:, columns(2, h)] = dot(hot[lines(h)], whole).astype(bf16)
    taken(2).wait_recv()

    def finish(d):
        ask(d).wait_send()
        send_page(d).wait_send()
        send_t(d).wait_send()
        return 0

    def close():
        each(1, n, finish)
        for j in range(3):
            give(j).wait_send()
            stores[j].wait()

    return close


def whole_kernel(
    n, g, depth, split, by_rows, counts, pages_at, tiles_at, offs_at, w1_at, w2_at,
    off_row, req, label_page, labels, out_a, out_t, out_aat, grad1, grad2,
    w1, w2, feats, sel, *rest,
):
    train, spread = rest[: counts[0]], rest[counts[0] :]
    early, late = training(
        g, depth, split, by_rows, feats, sel, w1, w2, labels, grad1, grad2, *train
    )
    close = propagate(
        n, pages_at, tiles_at, offs_at, w1_at, w2_at, off_row, req, label_page,
        out_a, out_t, out_aat, *spread[:6], w1, w2, feats, sel, *spread[6:], early,
    )
    late(close)


def trained(pages, band_tiles, off_tiles, off_row, requests, label_page, labels, w_first, w_second):
    n = lax.axis_size("band")
    g = max(1, round((n / 2) ** (1 / 3)))
    if n % (g * g):
        g = 1
    depth = n // (g * g)
    hid, classes = w_second.shape
    tile = band_tiles.shape[-1]
    rows, fh = pages.shape
    nb = rows // tile
    count = labels.shape[0]
    in_f = w_first.shape[0]
    top, low = in_f // 2, hid // 2
    picks = top // fh
    half = (w_first.size + w_second.size) // (2 * hid)
    rows2 = half // (g * g)
    by_rows = rows2 % (16 * depth) == 0
    chunks = max(1, hid // 256 if by_rows else hid // (128 * depth))
    broad = hid // chunks
    split = SPLIT if by_rows else 1
    pieces, width = chunks * split, broad // split
    f32, bf16, i16 = jnp.float32, jnp.bfloat16, jnp.int16
    tall, thin = (rows2 // depth, width) if by_rows else (rows2, width // depth)
    vmem = pl.BlockSpec(memory_space=pltpu.VMEM)
    smem = pl.BlockSpec(memory_space=pltpu.SMEM)
    anywhere = pl.BlockSpec(memory_space=pl.ANY)
    dma = pltpu.SemaphoreType.DMA
    side, deep = max(1, g - 1), max(1, depth - 1)
    near, far = dma((pieces, side)), dma((pieces, deep))
    first = pltpu.VMEM((pieces, side, half // g + 16, width), i16)
    second = pltpu.VMEM((pieces, side, rows2 + 16, width), i16)
    third = pltpu.VMEM((pieces, deep, tall, thin), i16)
    powers = pltpu.VMEM((pieces, deep, 1, thin), f32)
    blocks = jax.ShapeDtypeStruct((nb, tile, fh), bf16)
    slots, blocked = pltpu.SMEM((n,), jnp.int32), pltpu.SMEM((nb,), jnp.int32)
    per_band = pltpu.VMEM((n, tile, fh), bf16)
    padded = pltpu.VMEM((nb + 2, tile, fh), bf16)
    train = [
        pltpu.VMEM((2, chunks, half, broad), bf16),
        pltpu.VMEM((top, 2 * count), bf16),
        pltpu.VMEM((count, hid), bf16),
        pltpu.VMEM((count, low), bf16),
        pltpu.VMEM((2, count, classes), bf16),
        pltpu.VMEM((chunks, 2, count, broad), bf16),
        pltpu.VMEM((count, hid), f32),
        pltpu.VMEM((chunks, half, broad), f32),
        first, first, second, second, third, third, powers, powers,
        dma((2,)), dma((2,)), dma((chunks,)), dma((chunks,)),
        near, near, near, near, far, far, far, far, far, far, near, near, near, near,
        dma((pieces,)), dma((pieces,)),
        dma((2, chunks, picks + max(1, broad // classes))),
    ]
    held = pltpu.VMEM((nb, tile, fh), bf16)
    prop_a, prop_t, prop_aat, grad1, grad2 = pl.pallas_call(
        functools.partial(whole_kernel, n, g, depth, split, by_rows, (len(train),)),
        out_shape=(
            blocks, blocks, blocks,
            jax.ShapeDtypeStruct(w_first.shape, bf16),
            jax.ShapeDtypeStruct(w_second.shape, bf16),
        ),
        in_specs=[anywhere] * 5 + [smem, smem, vmem, vmem],
        out_specs=(anywhere,) * 5,
        scratch_shapes=[
            pltpu.VMEM(w_first.shape, bf16),
            pltpu.VMEM(w_second.shape, bf16),
            pltpu.VMEM((count, in_f), bf16),
            pltpu.VMEM((picks, count, fh), bf16),
            *train,
            held, held, held, held,
            pltpu.VMEM(band_tiles.shape, bf16),
            pltpu.VMEM(off_tiles.shape, bf16),
            pltpu.VMEM((2 * count, rows), bf16),
            pltpu.VMEM((n + 1, tile, fh), f32),
            per_band, per_band, per_band, per_band, per_band,
            padded, padded,
            pltpu.VMEM((2, tile, fh), f32),
            pltpu.VMEM((2, tile, fh), f32),
            pltpu.VMEM((nb, tile, fh), f32),
            pltpu.VMEM((nb, tile, fh), f32),
            pltpu.VMEM((n, 1, 128), jnp.int32),
            pltpu.VMEM((n, 1, 128), jnp.int32),
            pltpu.SMEM((n, 1, 128), jnp.int32),
            slots, slots, blocked, slots, slots, blocked,
            dma((8,)), dma((1,)),
            *([dma((n,))] * 8), dma((6,)), dma((6,)), dma((picks,)), dma((picks,)),
        ],
        compiler_params=pltpu.CompilerParams(
            collective_id=0, has_side_effects=True, vmem_limit_bytes=(58 if n <= 16 else 62) * 2**20
        ),
        name="train",
    )(
        pages.reshape(nb, tile, fh),
        band_tiles,
        off_tiles,
        w_first,
        w_second,
        off_row,
        requests,
        label_page.reshape(2 * count // 128, 1, 128),
        labels.reshape(count // 128, 1, 128),
    )
    return (
        prop_a.reshape(rows, fh), prop_t.reshape(rows, fh), prop_aat.reshape(rows, fh), grad1, grad2
    )


def hand_out(*refs):
    sources, targets, held, come, leave = refs[:5], refs[5:10], refs[10:15], refs[15], refs[16]
    steps = []
    for i, (source, target, middle) in enumerate(zip(sources, targets, held)):
        size = source.shape[0] // 2
        for j in range(2):
            rows = pl.ds(j * size, size)
            steps.append(
                (
                    pltpu.make_async_copy(source.at[rows], middle.at[rows], come.at[i, j]),
                    pltpu.make_async_copy(middle.at[rows], target.at[rows], leave.at[i, j]),
                )
            )
    for first, _ in steps:
        first.start()
    for first, second in steps:
        first.wait()
        second.start()
    for _, second in steps:
        second.wait()


def handed_out(*arrays):
    anywhere = pl.BlockSpec(memory_space=pl.ANY)
    dma = pltpu.SemaphoreType.DMA
    return pl.pallas_call(
        hand_out,
        out_shape=tuple(jax.ShapeDtypeStruct(a.shape, a.dtype) for a in arrays),
        in_specs=[anywhere] * 5,
        out_specs=(anywhere,) * 5,
        scratch_shapes=[
            *(pltpu.VMEM(a.shape, a.dtype) for a in arrays), dma((5, 2)), dma((5, 2))
        ],
        name="hand_out",
    )(*arrays)


def per_device(
    pages, band_tiles, off_tiles, off_row, requests, label_page, labels, w_first, w_second
):
    results = trained(
        pages, band_tiles, off_tiles, off_row, requests, label_page, labels, w_first, w_second
    )
    return handed_out(*results)


def solution(mesh):
    placed = (
        P("band", "dp"),
        P("band", None, None, None),
        P("band", None, None),
        P("band"),
        P("band"),
        P("band"),
        P(("band", "dp")),
        P(),
        P(),
    )
    return jax.shard_map(
        per_device,
        mesh=mesh,
        in_specs=placed,
        out_specs=(P("band", "dp"), P("band", "dp"), P("band", "dp"), P(), P()),
        check_vma=False,
    )
```
